32 devices in a mesh: lat: 8 (over z, core), lon: 4 (over y, x).
Axes of the slice: x: 2, y: 2, z: 4, core: 2. Of those that a mesh axis runs over, the one named last changes fastest.
Arguments:
- ensemble: float32 [80, 1, 256, 512], P(None, None, 'lat', 'lon'), may hold values from -6 to 6
- obs_value: float32 [4, 8, 4, 128], P(None, 'lat', 'lon'), may hold values from -6 to 6
- obs_error: float32 [4, 8, 4, 128], P(None, 'lat', 'lon'), may hold values from 0.25 to 4
- obs_cell: int32 [4, 8, 4, 128], P(None, 'lat', 'lon'), may hold values from 0 to 4095
- obs_radius: int32 [4, 8, 4, 128], P(None, 'lat', 'lon'), may hold values from 8 to 32
- obs_count: int32 [4, 8, 4], P(None, 'lat', 'lon'), may hold values from 16 to 128, as said below
- batch_order: int32 [4], replicated, may hold values from 0 to 3, each once
Outputs:
- analysis: float32 [80, 1, 256, 512], P(None, None, 'lat', 'lon')
The draws below stay inside these ranges and needn't reach their ends.
Inputs may be any that keep to these rules, and one draw needn't show every extreme that they name: `obs_count`: slots at or beyond the count hold no observation and are ignored. In every batch some tile has all 128 slots live.
All inputs are finite; a program needn't handle non-finite values.
Results may differ from the reference program's by a relative error of at most 0.0021.
Values may be sent and summed in bfloat16 or wider, within the bound.
A program may use at most 64 MiB of HBM per device.

```python
import math
import jax
import jax.numpy as jnp
from jax import lax

M = 80
LEV = 1
CLAT = 32
CLON = 128
CAP = 128
NB = 4
RMAX = 32
NLAT = 256
NLON = 512
N_LAT = 8
N_LON = 4


def draw_obs_count(key, part):
    first_key, second_key = jax.random.split(jax.random.fold_in(key, 17))
    halvings = jax.random.randint(first_key, (NB, N_LAT, N_LON), 0, 4)
    full_tile = jax.random.randint(second_key, (NB, 1, 1), 0, N_LAT * N_LON)
    tile_ids = jnp.arange(N_LAT, dtype=jnp.int32)[:, None] * N_LON + jnp.arange(N_LON, dtype=jnp.int32)[None, :]
    halvings = jnp.where(tile_ids[None] == full_tile, 0, halvings)
    return jnp.right_shift(jnp.full((NB, N_LAT, N_LON), CAP, jnp.int32), halvings.astype(jnp.int32)).astype(jnp.int32)


def place_ends(array, stream_key, least, top_value):
    dims = array.shape
    index_at = [jax.random.randint(jax.random.fold_in(stream_key, axis), (), 0, dims[axis]) for axis in range(len(dims))]
    array = array.at[tuple(index_at)].set(least)
    longest = dims.index(max(dims))
    index_at[longest] = (index_at[longest] + 1) % dims[longest]
    return array.at[tuple(index_at)].set(top_value)


def block_scale(own_key, extent, shards, smallest, largest):
    level = 1.0
    for position, parts in shards:
        heights = jax.random.uniform(jax.random.fold_in(jax.random.fold_in(own_key, 6), position), (parts,), jnp.float32, smallest / len(shards), largest / len(shards))
        level = level * jnp.repeat(jnp.exp(heights), extent[position] // parts).reshape((-1,) + (1,) * (len(extent) - 1 - position))
    return level


def scatter_about(own_key, shape, deviation, most, shards=(), kind=jnp.bfloat16):
    array = deviation * jax.random.normal(own_key, shape, jnp.float32)
    if shards:
        array = array * block_scale(own_key, shape, shards, -0.22, 0.18)
    return jnp.clip(array, -most, most).astype(kind)


def setup_inputs(seed: int = 0) -> dict:
    streams_of = jax.random.split(jax.random.key(seed), 8)
    return {
        "ensemble": scatter_about(streams_of[0], (M, LEV, NLAT, NLON), 1.0, 6.0, ((2, 8), (3, 4)), jnp.float32),
        "obs_value": scatter_about(streams_of[1], (NB, N_LAT, N_LON, CAP), 1.0, 6.0, ((1, 8), (2, 4)), jnp.float32),
        "obs_error": jnp.clip(jnp.exp(math.log(4.0) - 2.7725887 * jax.random.uniform(streams_of[2], (NB, N_LAT, N_LON, CAP), jnp.float32) ** block_scale(streams_of[2], (NB, N_LAT, N_LON, CAP), ((1, 8), (2, 4)), -0.2, 0.2)), 0.25, 4.0),
        "obs_cell": place_ends(jax.random.randint(streams_of[3], (NB, N_LAT, N_LON, CAP), 0, CLAT * CLON), jax.random.fold_in(streams_of[3], 1), 0, (CLAT * CLON) - 1).astype(jnp.int32),
        "obs_radius": place_ends(jax.random.randint(streams_of[4], (NB, N_LAT, N_LON, CAP), RMAX // 4, RMAX + 1), jax.random.fold_in(streams_of[4], 1), RMAX // 4, RMAX).astype(jnp.int32),
        "obs_count": draw_obs_count(jax.random.fold_in(streams_of[7], 71), 0),
        "batch_order": jax.random.permutation(streams_of[6], NB).astype(jnp.int32),
    }


def observe_stats(priors, values, errors, is_live):
    members = priors.shape[0]
    prior_mean = lax.optimization_barrier(jnp.mean(priors, axis=0))
    spread = priors - prior_mean
    variance = lax.optimization_barrier(jnp.sum(spread * spread, axis=0)) / (members - 1)
    denom_total = variance + errors
    shrink = 1.0 / (1.0 + jnp.sqrt(errors / denom_total))
    factor = 1.0 / ((members - 1) * denom_total)
    obs_pert = jnp.where(is_live, spread, 0.0).astype(jnp.bfloat16)
    obs_gain = jnp.where(is_live, factor * (values - prior_mean - shrink * spread), 0.0).astype(jnp.bfloat16)
    return (obs_pert, obs_gain)

def assimilate(current, obs_pert, obs_gain, where_ints, lat_base, lon_base, full_lon, block_cols):
    members, levels, lat_rows, lon_cols = current.shape
    cells = lat_rows * lon_cols
    flat_state = current.reshape(members, levels, cells)
    centered = (flat_state - lax.optimization_barrier(jnp.mean(flat_state, axis=0))).astype(jnp.bfloat16)
    obs_lat = where_ints[0]
    obs_lon = where_ints[1]
    cutoff = where_ints[2]
    cutoff_sq = cutoff * cutoff
    width_sq = jnp.maximum(cutoff_sq, 1).astype(jnp.float32)

    def one_block(block_id, total_inc):
        first_col = block_id * block_cols
        positions = first_col + jnp.arange(block_cols, dtype=jnp.int32)
        cell_lat = lat_base + positions // lon_cols
        cell_lon = lon_base + positions % lon_cols
        lat_gap = cell_lat[:, None] - obs_lat[None, :]
        lon_gap = jnp.abs(cell_lon[:, None] - obs_lon[None, :])
        lon_dist = jnp.minimum(lon_gap, full_lon - lon_gap)
        dist_sq = lat_gap * lat_gap + lon_dist * lon_dist
        weights = jnp.where(dist_sq <= cutoff_sq[None, :], jnp.exp(-2.0 * dist_sq.astype(jnp.float32) / width_sq[None, :]), 0.0)
        centered_block = lax.dynamic_slice_in_dim(centered, first_col, block_cols, 2).reshape(members, levels * block_cols)
        covariance = lax.dot_general(centered_block, obs_pert, (((0,), (0,)), ((), ())), preferred_element_type=jnp.float32)
        scaled = (covariance.reshape(levels, block_cols, -1) * weights[None]).astype(jnp.bfloat16).reshape(levels * block_cols, -1)
        increment = lax.dot_general(obs_gain, scaled, (((1,), (1,)), ((), ())), preferred_element_type=jnp.float32)
        return lax.dynamic_update_slice_in_dim(total_inc, increment.reshape(members, levels, block_cols), first_col, 2)
    total_inc = lax.fori_loop(0, cells // block_cols, one_block, jnp.zeros_like(flat_state))
    return (flat_state + total_inc).reshape(current.shape)

def neighbors(packed):
    padded = jnp.pad(packed, ((0, 0), (1, 1), (0, 0), (0, 0)))
    pieces = []
    for lat_move in (1, 0, -1):
        lat_band = padded[:, 1 - lat_move:1 - lat_move + N_LAT]
        for lon_move in (1, 0, -1):
            pieces.append(jnp.roll(lat_band, lon_move, axis=2))
    return jnp.concatenate(pieces, axis=3)

def reference(ensemble, obs_value, obs_error, obs_cell, obs_radius, obs_count, batch_order):
    tile_total = N_LAT * N_LON
    tile_ids = jnp.arange(tile_total, dtype=jnp.int32)
    tile_lat = tile_ids // N_LON * CLAT
    tile_lon = tile_ids % N_LON * CLON
    lat_start = (jnp.arange(N_LAT, dtype=jnp.int32) * CLAT)[:, None, None]
    lon_start = (jnp.arange(N_LON, dtype=jnp.int32) * CLON)[None, :, None]
    slot_ids = jnp.arange(CAP, dtype=jnp.int32)[None, None, :]
    current = ensemble
    for batch_step in range(NB):
        chosen = batch_order[batch_step]
        cell_ids = obs_cell[chosen]
        obs_lat = (lat_start + cell_ids // CLON).astype(jnp.int32)
        obs_lon = (lon_start + cell_ids % CLON).astype(jnp.int32)
        priors = current[:, 0][:, obs_lat, obs_lon]
        is_live = slot_ids < obs_count[chosen][:, :, None]
        obs_pert, obs_gain = observe_stats(priors, obs_value[chosen], obs_error[chosen], is_live)
        where_ints = jnp.stack([obs_lat, obs_lon, obs_radius[chosen]]).astype(jnp.int32)
        pert_near = neighbors(obs_pert).transpose(1, 2, 0, 3).reshape(tile_total, M, 9 * CAP)
        gain_near = neighbors(obs_gain).transpose(1, 2, 0, 3).reshape(tile_total, M, 9 * CAP)
        ints_near = neighbors(where_ints).transpose(1, 2, 0, 3).reshape(tile_total, 3, 9 * CAP)
        tile_blocks = current.reshape(M, LEV, N_LAT, CLAT, N_LON, CLON).transpose(2, 4, 0, 1, 3, 5).reshape(tile_total, M, LEV, CLAT, CLON)

        def tile_step(operands):
            one_tile, pert_tile, gain_tile, ints_tile, lat_base, lon_base = operands
            return assimilate(one_tile, pert_tile, gain_tile, ints_tile, lat_base, lon_base, NLON, CLAT * CLON)
        updated = lax.map(tile_step, (tile_blocks, pert_near, gain_near, ints_near, tile_lat, tile_lon))
        current = updated.reshape(N_LAT, N_LON, M, LEV, CLAT, CLON).transpose(2, 3, 0, 4, 1, 5).reshape(M, LEV, NLAT, NLON)
    return current
```

```python
import functools

import jax
import jax.numpy as jnp
from jax import lax
from jax.experimental import pallas as pl
from jax.experimental.pallas import tpu as pltpu
from jax.sharding import PartitionSpec as P

REACH = 32
LANES = 128
COL_BITS = 7
REACH_BITS = 5
TAIL = 16
UNROLL = 8
GROUP = 8

OFFSETS = ((0, 0), (-1, 0), (1, 0), (0, -1), (-1, -1), (1, -1), (0, 1), (-1, 1), (1, 1))
NORTH, SOUTH, WEST, EAST = 1, 2, 3, 6
CORNERS = (4, 5, 7, 8)
OUTGOING = (WEST, EAST) + CORNERS + (NORTH, SOUTH)


def repeat(count, unroll, body):
    def step(i, carry):
        for j in range(unroll):
            body(i * unroll + j)
        return carry

    lax.fori_loop(0, count // unroll, step, 0)


def opposite(slot):
    dy, dx = OFFSETS[slot]
    return OFFSETS.index((-dy, -dx))


def kernel(
    dims,
    x_hbm,
    value_hbm,
    error_hbm,
    cell_hbm,
    radius_hbm,
    count_hbm,
    order_hbm,
    out_ref,
    x_ref,
    value_ref,
    error_ref,
    cell_ref,
    radius_ref,
    cell_s,
    count_s,
    order_s,
    xt,
    cent,
    hx,
    packets,
    hp_all,
    gain_all,
    reach_lat,
    decay_lat,
    gap_mid,
    decay_mid,
    gap_side,
    decay_side,
    copy_sem,
    send_sem,
    recv_sem,
):
    members, rows, cols, slots, batches, n_lat, n_lon = dims
    padded = xt.shape[1]
    chunks = cols // REACH
    chunk_cells = rows * REACH
    row_groups = rows // GROUP
    block = GROUP * REACH
    f32, bf16 = jnp.float32, jnp.bfloat16
    lat = lax.axis_index("lat")
    lon = lax.axis_index("lon")
    has_north = lat > 0
    has_south = lat < n_lat - 1

    def device(slot):
        dy, dx = OFFSETS[slot]
        return (lat + dy, lax.rem(lon + dx + n_lon, n_lon))

    def at(slots_, action):
        for sign, present in ((0, None), (-1, has_north), (1, has_south)):
            chosen = [slot for slot in slots_ if OFFSETS[slot][0] == sign]
            if not chosen:
                continue
            if present is None:
                for slot in chosen:
                    action(slot)
            else:

                @pl.when(present)
                def _():
                    for slot in chosen:
                        action(slot)

    packets[...] = jnp.zeros_like(packets)
    barrier = pltpu.get_barrier_semaphore()

    def greet(slot):
        pl.semaphore_signal(
            barrier, inc=1, device_id=device(slot), device_id_type=pl.DeviceIdType.MESH
        )

    at(OUTGOING, greet)

    loads = [
        pltpu.make_async_copy(source, target, copy_sem.at[i])
        for i, (source, target) in enumerate(
            (
                (x_hbm, x_ref),
                (order_hbm, order_s),
                (count_hbm, count_s),
                (cell_hbm, cell_s),
                (value_hbm, value_ref),
                (error_hbm, error_ref),
                (cell_hbm, cell_ref),
                (radius_hbm, radius_ref),
            )
        )
    ]
    for load in loads:
        load.start()

    hp_all[...] = jnp.zeros_like(hp_all)
    gain_all[...] = jnp.zeros_like(gain_all)
    for load in loads:
        load.wait()

    def load_row(r):
        v = x_ref[pl.ds(r, members, stride=rows), :]
        mean = jnp.sum(v, axis=0, keepdims=True) * (1.0 / members)
        filler = jnp.where(
            lax.broadcasted_iota(jnp.int32, (padded - members, cols), 0) == 0, mean, 0.0
        )
        vt = jnp.transpose(jnp.concatenate([v - mean, filler], axis=0))
        vc = vt.astype(bf16)
        for q in range(chunks):
            start = pl.multiple_of(q * chunk_cells + r * REACH, REACH)
            xt[pl.ds(start, REACH), :] = vt[q * REACH : (q + 1) * REACH]
            cent[pl.ds(start, REACH), :] = vc[q * REACH : (q + 1) * REACH]

    repeat(rows, 8, load_row)

    above = (lat + n_lat - 1) // n_lat
    below = (2 * n_lat - 2 - lat) // n_lat
    pl.semaphore_wait(barrier, 2 + 3 * above + 3 * below)

    def outgoing(k, slot):
        return pltpu.make_async_remote_copy(
            src_ref=packets.at[k, 0],
            dst_ref=packets.at[k, opposite(slot)],
            send_sem=send_sem.at[k, slot],
            recv_sem=recv_sem.at[k, opposite(slot)],
            device_id=device(slot),
            device_id_type=pl.DeviceIdType.MESH,
        )

    def incoming(k, slot):
        return pltpu.make_async_remote_copy(
            src_ref=packets.at[k, 0],
            dst_ref=packets.at[k, slot],
            send_sem=send_sem.at[k, slot],
            recv_sem=recv_sem.at[k, slot],
            device_id=device(EAST),
            device_id_type=pl.DeviceIdType.MESH,
        )

    def unpack(k, slot):
        dy, dx = OFFSETS[slot]
        lanes = slice(slot * slots, (slot + 1) * slots)
        packet = packets[k, slot]
        hp = packet[:members]
        tail = packet[members:].astype(f32)
        radius = tail[3:4]
        scale = tail[4:5] + tail[5:6]
        hp_all[:members, lanes] = hp
        gain_all[:members, lanes] = hp
        first_row = lax.broadcasted_iota(jnp.int32, (TAIL, slots), 0) == 0
        gain_all[members : members + TAIL, lanes] = jnp.where(first_row, tail, 0.0).astype(bf16)
        reach2 = radius * radius
        rate = -2.0 / jnp.maximum(reach2, 1.0)
        row_ids = lax.broadcasted_iota(jnp.int32, (rows, slots), 0).astype(f32)
        dlat = row_ids - (tail[1:2] + float(dy * rows))
        dlat2 = dlat * dlat
        reach_lat[:, lanes] = reach2 - dlat2
        decay_lat[:, lanes] = jnp.exp(dlat2 * rate) * scale
        if dx == 0:
            col_ids = lax.broadcasted_iota(jnp.int32, (cols, slots), 0).astype(f32)
            dlon = col_ids - tail[2:3]
            gap_ref, decay_ref, here = gap_mid, decay_mid, lanes
        else:
            first = 0 if dx < 0 else cols - REACH
            col_ids = lax.broadcasted_iota(jnp.int32, (REACH, slots), 0).astype(f32)
            dlon = col_ids + float(first - dx * cols) - tail[2:3]
            gap_ref, decay_ref = gap_side, decay_side
            here = slice((slot - 3) * slots, (slot - 2) * slots)
        dlon2 = dlon * dlon
        gap_ref[:, here] = dlon2
        decay_ref[:, here] = jnp.exp(dlon2 * rate)

    def update(q, group, first_slot, n_slots, side, centring):
        lanes = slice(first_slot * slots, (first_slot + n_slots) * slots)
        cells = pl.ds(pl.multiple_of(q * chunk_cells + group * block, block), block)
        cov = jnp.dot(cent[cells, :], hp_all[:, lanes], preferred_element_type=f32)
        if side:
            here = slice((first_slot - 3) * slots, (first_slot - 3 + n_slots) * slots)
            gap, decay = gap_side[:, here], decay_side[:, here]
        else:
            columns = pl.ds(pl.multiple_of(q * REACH, REACH), REACH)
            gap, decay = gap_mid[columns, lanes], decay_mid[columns, lanes]
        lat_rows = pl.ds(pl.multiple_of(group * GROUP, GROUP), GROUP)
        reach = reach_lat[lat_rows, lanes]
        fade = decay_lat[lat_rows, lanes]
        parts = []
        for r in range(GROUP):
            weight = jnp.where(gap <= reach[r : r + 1], decay * fade[r : r + 1], 0.0)
            parts.append((cov[r * REACH : (r + 1) * REACH] * weight).astype(bf16))
        scaled = jnp.concatenate(parts, axis=0)
        inc = lax.dot_general(
            scaled, gain_all[:, lanes], (((1,), (1,)), ((), ())), preferred_element_type=f32
        )
        x = xt[cells, :] + inc
        xt[cells, :] = x
        if centring:
            cent[cells, :] = x.astype(bf16)

    def sweep(first_q, n_q, first_slot, n_slots, side=False, centring=False):
        def step(i):
            q = first_q + i // row_groups
            update(q, i % row_groups, first_slot, n_slots, side, centring)

        repeat(n_q * row_groups, min(UNROLL, n_q * row_groups), step)

    def one_batch(k, carry):
        chosen = order_s[k]

        def gather(i, inner):
            for j in range(16):
                s = i * 16 + j
                cell = cell_s[chosen, 0, 0, s]
                chunk = (cell & (cols - 1)) >> REACH_BITS
                row = cell >> COL_BITS
                place = chunk * chunk_cells + row * REACH + (cell & (REACH - 1))
                hx[pl.ds(s, 1), :] = xt[pl.ds(place, 1), :]
            return inner

        lax.fori_loop(0, slots // 16, gather, 0)
        prior = jnp.transpose(hx[...])
        pert = prior[:members]
        mean = prior[members : members + 1]
        var = jnp.sum(pert * pert, axis=0, keepdims=True) * (1.0 / (members - 1))
        error = error_ref[chosen, 0]
        total = var + error
        spread = 1.0 + jnp.sqrt(error / total)
        live = lax.broadcasted_iota(jnp.int32, (1, slots), 1) < count_s[0, 0, chosen]
        scale = jnp.where(live, -1.0 / (((members - 1) * total) * spread), 0.0)
        shift = jnp.where(live, (mean - value_ref[chosen, 0]) * spread, 0.0)
        high = scale.astype(bf16).astype(f32)
        cell = cell_ref[chosen, 0]
        tail = jnp.concatenate(
            [
                shift,
                (cell >> COL_BITS).astype(f32),
                (cell & (cols - 1)).astype(f32),
                radius_ref[chosen, 0].astype(f32),
                high,
                scale - high,
                jnp.zeros((TAIL - 6, slots), f32),
            ],
            axis=0,
        )
        packets[k, 0, :members, :] = jnp.where(live, pert, 0.0).astype(bf16)
        packets[k, 0, members:, :] = tail.astype(bf16)
        at(OUTGOING, lambda slot: outgoing(k, slot).start())

        unpack(k, 0)
        sweep(0, chunks, 0, 1)

        at((NORTH, SOUTH), lambda slot: incoming(k, slot).wait_recv())
        for slot in (NORTH, SOUTH):
            unpack(k, slot)
        sweep(1, chunks - 2, 1, 2, centring=True)
        sweep(0, 1, 1, 2)
        sweep(chunks - 1, 1, 1, 2)

        at((WEST, EAST), lambda slot: incoming(k, slot).wait_recv())
        for slot in (WEST, EAST):
            unpack(k, slot)
        sweep(0, 1, WEST, 1, side=True)
        sweep(chunks - 1, 1, EAST, 1, side=True)

        at(CORNERS, lambda slot: incoming(k, slot).wait_recv())
        for slot in CORNERS:
            unpack(k, slot)
        sweep(0, 1, WEST + 1, 2, side=True, centring=True)
        sweep(chunks - 1, 1, EAST + 1, 2, side=True, centring=True)
        return carry

    lax.fori_loop(0, batches, one_batch, 0)

    def store_row(r):
        pieces = [
            xt[pl.ds(pl.multiple_of(q * chunk_cells + r * REACH, REACH), REACH), :]
            for q in range(chunks)
        ]
        v = jnp.transpose(jnp.concatenate(pieces, axis=0))
        out_ref[pl.ds(r, members, stride=rows), :] = v[:members] + v[members : members + 1]

    repeat(rows, 8, store_row)

    def finish(k, carry):
        at(OUTGOING, lambda slot: outgoing(k, slot).wait_send())
        return carry

    lax.fori_loop(0, batches, finish, 0)


def local(ensemble, obs_value, obs_error, obs_cell, obs_radius, obs_count, batch_order):
    members, levels, rows, cols = ensemble.shape
    batches = obs_cell.shape[0]
    slots = obs_cell.shape[-1]
    assert levels == 1 and cols == LANES and slots == LANES and rows == REACH
    n_lat, n_lon = lax.axis_size("lat"), lax.axis_size("lon")
    padded = -(-members // LANES) * LANES
    cells = rows * cols
    tiles = len(OFFSETS)
    vmem = pl.BlockSpec(memory_space=pltpu.VMEM)
    hbm = pl.BlockSpec(memory_space=pltpu.HBM)
    f32, bf16, i32 = jnp.float32, jnp.bfloat16, jnp.int32
    small = (batches, 1, 1, slots)
    out = pl.pallas_call(
        functools.partial(kernel, (members, rows, cols, slots, batches, n_lat, n_lon)),
        out_shape=pltpu.VMEM((members * rows, cols), f32),
        in_specs=[hbm] * 7,
        out_specs=vmem,
        scratch_shapes=[
            pltpu.VMEM((members * rows, cols), f32),
            pltpu.VMEM(small, f32),
            pltpu.VMEM(small, f32),
            pltpu.VMEM(small, i32),
            pltpu.VMEM(small, i32),
            pltpu.SMEM(small, i32),
            pltpu.SMEM((1, 1, batches), i32),
            pltpu.SMEM((batches,), i32),
            pltpu.VMEM((cells, padded), f32),
            pltpu.VMEM((cells, padded), bf16),
            pltpu.VMEM((slots, padded), f32),
            pltpu.VMEM((batches, tiles, members + TAIL, slots), bf16),
            pltpu.VMEM((padded, tiles * slots), bf16),
            pltpu.VMEM((padded, tiles * slots), bf16),
            pltpu.VMEM((rows, tiles * slots), f32),
            pltpu.VMEM((rows, tiles * slots), f32),
            pltpu.VMEM((cols, 3 * slots), f32),
            pltpu.VMEM((cols, 3 * slots), f32),
            pltpu.VMEM((REACH, 6 * slots), f32),
            pltpu.VMEM((REACH, 6 * slots), f32),
            pltpu.SemaphoreType.DMA((8,)),
            pltpu.SemaphoreType.DMA((batches, tiles)),
            pltpu.SemaphoreType.DMA((batches, tiles)),
        ],
        compiler_params=pltpu.CompilerParams(
            collective_id=0, has_side_effects=True, vmem_limit_bytes=58 * 1024 * 1024
        ),
    )(
        ensemble.reshape(members * rows, cols),
        obs_value,
        obs_error,
        obs_cell,
        obs_radius,
        jnp.transpose(obs_count, (1, 2, 0)),
        batch_order,
    )
    return out.reshape(ensemble.shape)


def solution(mesh):
    return jax.shard_map(
        local,
        mesh=mesh,
        in_specs=(
            P(None, None, "lat", "lon"),
            P(None, "lat", "lon", None),
            P(None, "lat", "lon", None),
            P(None, "lat", "lon", None),
            P(None, "lat", "lon", None),
            P(None, "lat", "lon"),
            P(),
        ),
        out_specs=P(None, None, "lat", "lon"),
        check_vma=False,
    )
```

```python
import functools

import jax
import jax.numpy as jnp
from jax import lax
from jax.experimental import pallas as pl
from jax.experimental.pallas import tpu as pltpu
from jax.sharding import PartitionSpec as P

REACH = 32
LANES = 128
COL_BITS = 7
REACH_BITS = 5
TAIL = 16
UNROLL = 8
GROUP = 8

OFFSETS = ((0, 0), (-1, 0), (1, 0), (0, -1), (-1, -1), (1, -1), (0, 1), (-1, 1), (1, 1))
NORTH, SOUTH, WEST, EAST = 1, 2, 3, 6
CORNERS = (4, 5, 7, 8)
SENDS = ((WEST, EAST), (NORTH, SOUTH), CORNERS)
NEIGHBOURS = (WEST, EAST, NORTH, SOUTH) + CORNERS


def repeat(count, unroll, body):
    def step(i, carry):
        for j in range(unroll):
            body(i * unroll + j)
        return carry

    lax.fori_loop(0, count // unroll, step, 0)


def opposite(slot):
    dy, dx = OFFSETS[slot]
    return OFFSETS.index((-dy, -dx))


def kernel(
    dims,
    x_hbm,
    value_hbm,
    error_hbm,
    cell_hbm,
    radius_hbm,
    count_hbm,
    order_hbm,
    out_ref,
    x_ref,
    value_ref,
    error_ref,
    cell_ref,
    radius_ref,
    cell_s,
    count_s,
    order_s,
    xt,
    cent,
    hx,
    hb,
    row_at,
    col_at,
    packets,
    hp_all,
    gain_all,
    reach_lat,
    decay_lat,
    gap_mid,
    decay_mid,
    gap_side,
    decay_side,
    copy_sem,
    send_sem,
    recv_sem,
):
    members, rows, cols, slots, batches, n_lat, n_lon = dims
    padded = xt.shape[1]
    chunks = cols // REACH
    chunk_cells = rows * REACH
    row_groups = rows // GROUP
    block = GROUP * REACH
    f32, bf16 = jnp.float32, jnp.bfloat16
    lat = lax.axis_index("lat")
    lon = lax.axis_index("lon")
    has_north = lat > 0
    has_south = lat < n_lat - 1

    def device(slot):
        dy, dx = OFFSETS[slot]
        return (lat + dy, lax.rem(lon + dx + n_lon, n_lon))

    def at(slots_, action):
        for sign, present in ((0, None), (-1, has_north), (1, has_south)):
            chosen = [slot for slot in slots_ if OFFSETS[slot][0] == sign]
            if not chosen:
                continue
            if present is None:
                for slot in chosen:
                    action(slot)
            else:

                @pl.when(present)
                def _():
                    for slot in chosen:
                        action(slot)

    barrier = pltpu.get_barrier_semaphore()

    def greet(slot):
        pl.semaphore_signal(
            barrier, inc=1, device_id=device(slot), device_id_type=pl.DeviceIdType.MESH
        )

    at(NEIGHBOURS, greet)

    loads = [
        pltpu.make_async_copy(source, target, copy_sem.at[i])
        for i, (source, target) in enumerate(
            (
                (x_hbm, x_ref),
                (order_hbm, order_s),
                (count_hbm, count_s),
                (cell_hbm, cell_s),
                (value_hbm, value_ref),
                (error_hbm, error_ref),
                (cell_hbm, cell_ref),
                (radius_hbm, radius_ref),
            )
        )
    ]
    for load in loads:
        load.start()

    for sign, present in ((-1, has_north), (1, has_south)):

        @pl.when(jnp.logical_not(present))
        def _():
            for slot in NEIGHBOURS:
                if OFFSETS[slot][0] == sign:
                    packets[:, slot] = jnp.zeros((batches,) + packets.shape[2:], bf16)

    hp_all[:, members:] = jnp.zeros((batches, padded - members, hp_all.shape[2]), bf16)
    gain_all[:, members:] = jnp.zeros((batches, padded - members, gain_all.shape[2]), bf16)
    for load in loads:
        load.wait()

    def load_row(r):
        v = x_ref[pl.ds(r, members, stride=rows), :]
        mean = jnp.sum(v, axis=0, keepdims=True) * (1.0 / members)
        filler = jnp.where(
            lax.broadcasted_iota(jnp.int32, (padded - members, cols), 0) == 0, mean, 0.0
        )
        vt = jnp.transpose(jnp.concatenate([v - mean, filler], axis=0))
        vc = vt.astype(bf16)
        for q in range(chunks):
            start = pl.multiple_of(q * chunk_cells + r * REACH, REACH)
            xt[pl.ds(start, REACH), :] = vt[q * REACH : (q + 1) * REACH]
            cent[pl.ds(start, REACH), :] = vc[q * REACH : (q + 1) * REACH]

    repeat(rows, 8, load_row)

    def outgoing(k, slot):
        return pltpu.make_async_remote_copy(
            src_ref=packets.at[k, 0],
            dst_ref=packets.at[k, opposite(slot)],
            send_sem=send_sem.at[k, slot],
            recv_sem=recv_sem.at[k, opposite(slot)],
            device_id=device(slot),
            device_id_type=pl.DeviceIdType.MESH,
        )

    def incoming(k, slot):
        return pltpu.make_async_remote_copy(
            src_ref=packets.at[k, 0],
            dst_ref=packets.at[k, slot],
            send_sem=send_sem.at[k, slot],
            recv_sem=recv_sem.at[k, slot],
            device_id=device(EAST),
            device_id_type=pl.DeviceIdType.MESH,
        )

    def unpack(k, slot):
        lanes = slice(slot * slots, (slot + 1) * slots)
        hp = packets[k, slot, :members, :]
        tail = packets[k, slot, members:, :].astype(f32)
        hp_all[k, :members, lanes] = hp
        gain_all[k, :members, lanes] = hp
        first_row = lax.broadcasted_iota(jnp.int32, (TAIL, slots), 0) == 0
        gain_all[k, members : members + TAIL, lanes] = jnp.where(first_row, tail, 0.0).astype(bf16)

    def place(k, slot):
        tail = packets[k, slot, members:, :].astype(f32)
        dy, dx = OFFSETS[slot]
        reach2 = tail[3:4] * tail[3:4]
        rate = -2.0 / jnp.maximum(reach2, 1.0)
        return tail[1:2] + float(dy * rows), tail[2:3] + float(dx * cols), reach2, rate, tail[4:5] + tail[5:6]

    def tabulate(k, slot):
        lanes = slice(slot * slots, (slot + 1) * slots)
        row, col, reach2, rate, scale = place(k, slot)
        dx = OFFSETS[slot][1]
        dlat = lax.broadcasted_iota(jnp.int32, (rows, slots), 0).astype(f32) - row
        dlat2 = dlat * dlat
        reach_lat[k, :, lanes] = reach2 - dlat2
        decay_lat[k, :, lanes] = jnp.exp(dlat2 * rate) * scale
        if dx == 0:
            dlon = lax.broadcasted_iota(jnp.int32, (cols, slots), 0).astype(f32) - col
            gap_ref, decay_ref, here = gap_mid, decay_mid, lanes
        else:
            first = 0 if dx < 0 else cols - REACH
            dlon = lax.broadcasted_iota(jnp.int32, (REACH, slots), 0).astype(f32) + float(first) - col
            gap_ref, decay_ref = gap_side, decay_side
            here = slice((slot - 3) * slots, (slot - 2) * slots)
        dlon2 = dlon * dlon
        gap_ref[k, :, here] = dlon2
        decay_ref[k, :, here] = jnp.exp(dlon2 * rate)

    def update(k, q, group, first_slot, n_slots, side, centring):
        lanes = slice(first_slot * slots, (first_slot + n_slots) * slots)
        cells = pl.ds(pl.multiple_of(q * chunk_cells + group * block, block), block)
        cov = jnp.dot(cent[cells, :], hp_all[k, :, lanes], preferred_element_type=f32)
        if side:
            here = slice((first_slot - 3) * slots, (first_slot - 3 + n_slots) * slots)
            gap, decay = gap_side[k, :, here], decay_side[k, :, here]
        else:
            columns = pl.ds(pl.multiple_of(q * REACH, REACH), REACH)
            gap, decay = gap_mid[k, columns, lanes], decay_mid[k, columns, lanes]
        lat_rows = pl.ds(pl.multiple_of(group * GROUP, GROUP), GROUP)
        reach = reach_lat[k, lat_rows, lanes]
        fade = decay_lat[k, lat_rows, lanes]
        parts = []
        for r in range(GROUP):
            weight = jnp.where(gap <= reach[r : r + 1], decay * fade[r : r + 1], 0.0)
            parts.append((cov[r * REACH : (r + 1) * REACH] * weight).astype(bf16))
        scaled = jnp.concatenate(parts, axis=0)
        inc = lax.dot_general(
            scaled, gain_all[k, :, lanes], (((1,), (1,)), ((), ())), preferred_element_type=f32
        )
        x = xt[cells, :] + inc
        xt[cells, :] = x
        if centring:
            cent[cells, :] = x.astype(bf16)

    def sweep(k, first_q, n_q, first_slot, n_slots, side=False, centring=False):
        def step(i):
            q = first_q + i // row_groups
            update(k, q, i % row_groups, first_slot, n_slots, side, centring)

        repeat(n_q * row_groups, min(UNROLL, n_q * row_groups), step)

    def gather(k):
        chosen = order_s[k]

        def some(i, inner):
            for j in range(16):
                s = i * 16 + j
                cell = cell_s[chosen, 0, 0, s]
                chunk = (cell & (cols - 1)) >> REACH_BITS
                row = cell >> COL_BITS
                spot = chunk * chunk_cells + row * REACH + (cell & (REACH - 1))
                hx[pl.ds(s, 1), :] = xt[pl.ds(spot, 1), :]
            return inner

        lax.fori_loop(0, slots // 16, some, 0)

    def aim(k):
        cell = jnp.broadcast_to(cell_ref[order_s[k], 0], (slots, slots))
        at_cell = jnp.transpose(cell.astype(f32)).astype(jnp.int32)
        row_at[...] = (at_cell >> COL_BITS).astype(f32)
        col_at[...] = (at_cell & (cols - 1)).astype(f32)
        hb[...] = hx[...].astype(bf16)

    def look(k, first_slot, n_slots):
        lanes = slice(first_slot * slots, (first_slot + n_slots) * slots)
        cov = jnp.dot(hb[...], hp_all[k, :, lanes], preferred_element_type=f32)
        parts = []
        for i in range(n_slots):
            row, col, reach2, rate, scale = place(k, first_slot + i)
            dlat = row_at[...] - row
            dlon = col_at[...] - col
            gap = dlat * dlat + dlon * dlon
            weight = jnp.where(gap <= reach2, jnp.exp(gap * rate) * scale, 0.0)
            parts.append((cov[:, i * slots : (i + 1) * slots] * weight).astype(bf16))
        scaled = jnp.concatenate(parts, axis=1)
        hx[...] += lax.dot_general(
            scaled, gain_all[k, :, lanes], (((1,), (1,)), ((), ())), preferred_element_type=f32
        )

    def prepare(k):
        chosen = order_s[k]
        prior = jnp.transpose(hx[...])
        pert = prior[:members]
        mean = prior[members : members + 1]
        var = jnp.sum(pert * pert, axis=0, keepdims=True) * (1.0 / (members - 1))
        error = error_ref[chosen, 0]
        total = var + error
        spread = 1.0 + jnp.sqrt(error / total)
        live = lax.broadcasted_iota(jnp.int32, (1, slots), 1) < count_s[0, 0, chosen]
        scale = jnp.where(live, -1.0 / (((members - 1) * total) * spread), 0.0)
        shift = jnp.where(live, (mean - value_ref[chosen, 0]) * spread, 0.0)
        high = scale.astype(bf16).astype(f32)
        cell = cell_ref[chosen, 0]
        tail = jnp.concatenate(
            [
                shift,
                (cell >> COL_BITS).astype(f32),
                (cell & (cols - 1)).astype(f32),
                radius_ref[chosen, 0].astype(f32),
                high,
                scale - high,
                jnp.zeros((TAIL - 6, slots), f32),
            ],
            axis=0,
        )
        packets[k, 0, :members, :] = jnp.where(live, pert, 0.0).astype(bf16)
        packets[k, 0, members:, :] = tail.astype(bf16)

    def send(k):
        for group in SENDS:
            at(group, lambda slot: outgoing(k, slot).start())

    def receive(k, slots_):
        at(slots_, lambda slot: incoming(k, slot).wait_recv())
        for slot in slots_:
            unpack(k, slot)

    def sides(k):
        for slot in (WEST, EAST) + CORNERS:
            tabulate(k, slot)
        sweep(k, 0, 1, WEST, 3, side=True, centring=True)
        sweep(k, chunks - 1, 1, EAST, 3, side=True, centring=True)

    last = batches - 1

    def one_batch(k, carry):
        @pl.when(k > 0)
        def _():
            sides(k - 1)

        @pl.when(k < last)
        def _():
            gather(k + 1)
            aim(k + 1)

        unpack(k, 0)
        tabulate(k, 0)
        sweep(k, 0, chunks, 0, 1)

        receive(k, (NORTH, SOUTH))
        for slot in (NORTH, SOUTH):
            tabulate(k, slot)
        sweep(k, 1, chunks - 2, 1, 2, centring=True)
        sweep(k, 0, 1, 1, 2)
        sweep(k, chunks - 1, 1, 1, 2)

        @pl.when(k < last)
        def _():
            look(k, 0, 3)

        receive(k, (WEST, EAST))

        @pl.when(k < last)
        def _():
            look(k, WEST, 1)
            look(k, EAST, 1)
            receive(k, CORNERS)
            look(k, WEST + 1, 2)
            look(k, EAST + 1, 2)
            prepare(k + 1)
            send(k + 1)

        return carry

    gather(0)
    prepare(0)
    above = (lat + n_lat - 1) // n_lat
    below = (2 * n_lat - 2 - lat) // n_lat
    pl.semaphore_wait(barrier, 2 + 3 * above + 3 * below)
    send(0)
    lax.fori_loop(0, batches, one_batch, 0)

    for slot in (WEST, EAST):
        tabulate(last, slot)
    sweep(last, 0, 1, WEST, 1, side=True)
    sweep(last, chunks - 1, 1, EAST, 1, side=True)
    receive(last, CORNERS)
    for slot in CORNERS:
        tabulate(last, slot)
    sweep(last, 0, 1, WEST + 1, 2, side=True)
    sweep(last, chunks - 1, 1, EAST + 1, 2, side=True)

    def store_row(r):
        pieces = [
            xt[pl.ds(pl.multiple_of(q * chunk_cells + r * REACH, REACH), REACH), :]
            for q in range(chunks)
        ]
        v = jnp.transpose(jnp.concatenate(pieces, axis=0))
        out_ref[pl.ds(r, members, stride=rows), :] = v[:members] + v[members : members + 1]

    repeat(rows, 8, store_row)

    def finish(k, carry):
        at(NEIGHBOURS, lambda slot: outgoing(k, slot).wait_send())
        return carry

    lax.fori_loop(0, batches, finish, 0)


def local(ensemble, obs_value, obs_error, obs_cell, obs_radius, obs_count, batch_order):
    members, levels, rows, cols = ensemble.shape
    batches = obs_cell.shape[0]
    slots = obs_cell.shape[-1]
    assert levels == 1 and cols == LANES and slots == LANES and rows == REACH
    n_lat, n_lon = lax.axis_size("lat"), lax.axis_size("lon")
    padded = -(-members // LANES) * LANES
    cells = rows * cols
    tiles = len(OFFSETS)
    vmem = pl.BlockSpec(memory_space=pltpu.VMEM)
    hbm = pl.BlockSpec(memory_space=pltpu.HBM)
    f32, bf16, i32 = jnp.float32, jnp.bfloat16, jnp.int32
    small = (batches, 1, 1, slots)
    out = pl.pallas_call(
        functools.partial(kernel, (members, rows, cols, slots, batches, n_lat, n_lon)),
        out_shape=pltpu.VMEM((members * rows, cols), f32),
        in_specs=[hbm] * 7,
        out_specs=vmem,
        scratch_shapes=[
            pltpu.VMEM((members * rows, cols), f32),
            pltpu.VMEM(small, f32),
            pltpu.VMEM(small, f32),
            pltpu.VMEM(small, i32),
            pltpu.VMEM(small, i32),
            pltpu.SMEM(small, i32),
            pltpu.SMEM((1, 1, batches), i32),
            pltpu.SMEM((batches,), i32),
            pltpu.VMEM((cells, padded), f32),
            pltpu.VMEM((cells, padded), bf16),
            pltpu.VMEM((slots, padded), f32),
            pltpu.VMEM((slots, padded), bf16),
            pltpu.VMEM((slots, slots), f32),
            pltpu.VMEM((slots, slots), f32),
            pltpu.VMEM((batches, tiles, members + TAIL, slots), bf16),
            pltpu.VMEM((batches, padded, tiles * slots), bf16),
            pltpu.VMEM((batches, padded, tiles * slots), bf16),
            pltpu.VMEM((batches, rows, tiles * slots), f32),
            pltpu.VMEM((batches, rows, tiles * slots), f32),
            pltpu.VMEM((batches, cols, 3 * slots), f32),
            pltpu.VMEM((batches, cols, 3 * slots), f32),
            pltpu.VMEM((batches, REACH, 6 * slots), f32),
            pltpu.VMEM((batches, REACH, 6 * slots), f32),
            pltpu.SemaphoreType.DMA((8,)),
            pltpu.SemaphoreType.DMA((batches, tiles)),
            pltpu.SemaphoreType.DMA((batches, tiles)),
        ],
        compiler_params=pltpu.CompilerParams(
            collective_id=0, has_side_effects=True, vmem_limit_bytes=58 * 1024 * 1024
        ),
    )(
        ensemble.reshape(members * rows, cols),
        obs_value,
        obs_error,
        obs_cell,
        obs_radius,
        jnp.transpose(obs_count, (1, 2, 0)),
        batch_order,
    )
    return out.reshape(ensemble.shape)


def solution(mesh):
    return jax.shard_map(
        local,
        mesh=mesh,
        in_specs=(
            P(None, None, "lat", "lon"),
            P(None, "lat", "lon", None),
            P(None, "lat", "lon", None),
            P(None, "lat", "lon", None),
            P(None, "lat", "lon", None),
            P(None, "lat", "lon"),
            P(),
        ),
        out_specs=P(None, None, "lat", "lon"),
        check_vma=False,
    )
```

```python
import functools

import jax
import jax.numpy as jnp
from jax import lax
from jax.experimental import pallas as pl
from jax.experimental.pallas import tpu as pltpu
from jax.sharding import PartitionSpec as P

REACH = 32
LANES = 128
COL_BITS = 7
REACH_BITS = 5
TAIL = 16
LINES = 3
RADIUS_BITS = 6
RADIUS_SPAN = 1 << RADIUS_BITS
UNROLL = 16
GROUP = 16

OFFSETS = ((0, 0), (-1, 0), (1, 0), (0, -1), (-1, -1), (1, -1), (0, 1), (-1, 1), (1, 1))
NORTH, SOUTH, WEST, EAST = 1, 2, 3, 6
STACK = (NORTH, 2, False)
CORNERS = (4, 5, 7, 8)
SENDS = ((WEST, EAST), (NORTH, SOUTH), CORNERS)
NEIGHBOURS = (WEST, EAST, NORTH, SOUTH) + CORNERS


def repeat(count, unroll, body):
    def step(i, carry):
        for j in range(unroll):
            body(i * unroll + j)
        return carry

    lax.fori_loop(0, count // unroll, step, 0)


def opposite(slot):
    dy, dx = OFFSETS[slot]
    return OFFSETS.index((-dy, -dx))


def kernel(
    dims,
    x_hbm,
    value_hbm,
    error_hbm,
    cell_hbm,
    radius_hbm,
    count_hbm,
    order_hbm,
    out_ref,
    x_ref,
    value_ref,
    error_ref,
    cell_ref,
    radius_ref,
    spot_v,
    spot_s,
    count_s,
    order_s,
    xt,
    cent,
    hx,
    hb,
    row_at,
    col_at,
    packets,
    tails,
    hp_all,
    gain_all,
    reach_lat,
    decay_lat,
    gap_mid,
    decay_mid,
    gap_side,
    decay_side,
    copy_sem,
    send_sem,
    recv_sem,
    tail_send_sem,
    tail_recv_sem,
):
    members, rows, cols, slots, batches, n_lat, n_lon = dims
    padded = xt.shape[1]
    chunks = cols // REACH
    chunk_cells = rows * REACH
    row_groups = rows // GROUP
    block = GROUP * REACH
    f32, bf16 = jnp.float32, jnp.bfloat16
    lat = lax.axis_index("lat")
    lon = lax.axis_index("lon")
    has_north = lat > 0
    has_south = lat < n_lat - 1

    def device(slot):
        dy, dx = OFFSETS[slot]
        return (lat + dy, lax.rem(lon + dx + n_lon, n_lon))

    def at(slots_, action):
        for sign, present in ((0, None), (-1, has_north), (1, has_south)):
            chosen = [slot for slot in slots_ if OFFSETS[slot][0] == sign]
            if not chosen:
                continue
            if present is None:
                for slot in chosen:
                    action(slot)
            else:

                @pl.when(present)
                def _():
                    for slot in chosen:
                        action(slot)

    barrier = pltpu.get_barrier_semaphore()

    def greet(slot):
        pl.semaphore_signal(
            barrier, inc=1, device_id=device(slot), device_id_type=pl.DeviceIdType.MESH
        )

    at(NEIGHBOURS, greet)

    loads = [
        pltpu.make_async_copy(source, target, copy_sem.at[i])
        for i, (source, target) in enumerate(
            (
                (x_hbm, x_ref),
                (order_hbm, order_s),
                (count_hbm, count_s),
                (value_hbm, value_ref),
                (error_hbm, error_ref),
                (cell_hbm, cell_ref),
                (radius_hbm, radius_ref),
            )
        )
    ]
    for load in loads:
        load.start()

    for sign, present in ((-1, has_north), (1, has_south)):

        @pl.when(jnp.logical_not(present))
        def _():
            for slot in NEIGHBOURS:
                if OFFSETS[slot][0] == sign:
                    packets[:, slot] = jnp.zeros((batches,) + packets.shape[2:], bf16)
                    tails[:, slot] = jnp.zeros((batches,) + tails.shape[2:], f32)

    hp_all[:, members:] = jnp.zeros((batches, padded - members, hp_all.shape[2]), bf16)
    gain_all[:, members:] = jnp.zeros((batches, padded - members, gain_all.shape[2]), bf16)
    for load in loads:
        load.wait()
    cell = cell_ref[...]
    chunk = (cell & (cols - 1)) >> REACH_BITS
    spot_v[...] = chunk * chunk_cells + (cell >> COL_BITS) * REACH + (cell & (REACH - 1))
    spots = pltpu.make_async_copy(spot_v, spot_s, copy_sem.at[7])
    spots.start()

    def load_row(r):
        v = x_ref[pl.ds(r, members, stride=rows), :]
        mean = jnp.sum(v, axis=0, keepdims=True) * (1.0 / members)
        filler = jnp.where(
            lax.broadcasted_iota(jnp.int32, (padded - members, cols), 0) == 0, mean, 0.0
        )
        vt = jnp.transpose(jnp.concatenate([v - mean, filler], axis=0))
        vc = vt.astype(bf16)
        for q in range(chunks):
            start = pl.multiple_of(q * chunk_cells + r * REACH, REACH)
            xt[pl.ds(start, REACH), :] = vt[q * REACH : (q + 1) * REACH]
            cent[pl.ds(start, REACH), :] = vc[q * REACH : (q + 1) * REACH]

    repeat(rows, 8, load_row)

    def moves(k, source, target, sender, toward):
        lines = pl.ds(0, LINES)
        return (
            pltpu.make_async_remote_copy(
                src_ref=packets.at[k, source],
                dst_ref=packets.at[k, target],
                send_sem=send_sem.at[k, sender],
                recv_sem=recv_sem.at[k, target],
                device_id=device(toward),
                device_id_type=pl.DeviceIdType.MESH,
            ),
            pltpu.make_async_remote_copy(
                src_ref=tails.at[k, source, lines],
                dst_ref=tails.at[k, target, lines],
                send_sem=tail_send_sem.at[k, sender],
                recv_sem=tail_recv_sem.at[k, target],
                device_id=device(toward),
                device_id_type=pl.DeviceIdType.MESH,
            ),
        )

    def start(k, slot):
        for move in moves(k, 0, opposite(slot), slot, slot):
            move.start()

    def wait_sent(k, slot):
        for move in moves(k, 0, opposite(slot), slot, slot):
            move.wait_send()

    def wait_arrived(k, slot):
        for move in moves(k, 0, slot, slot, EAST):
            move.wait_recv()

    def unpack(k, slot):
        lanes = slice(slot * slots, (slot + 1) * slots)
        hp = packets[k, slot]
        hp_all[k, :members, lanes] = hp
        gain_all[k, :members, lanes] = hp
        first_row = lax.broadcasted_iota(jnp.int32, (TAIL, slots), 0) == 0
        shift = jnp.broadcast_to(tails[k, slot, 0:1, :], (TAIL, slots))
        gain_all[k, members : members + TAIL, lanes] = jnp.where(first_row, shift, 0.0).astype(bf16)

    def place(k, slot):
        dy, dx = OFFSETS[slot]
        code = tails[k, slot, 2:3, :].astype(jnp.int32)
        radius = (code & (RADIUS_SPAN - 1)).astype(f32)
        row = (code >> (RADIUS_BITS + COL_BITS)).astype(f32)
        col = ((code >> RADIUS_BITS) & (cols - 1)).astype(f32)
        reach2 = radius * radius
        rate = -2.0 / jnp.maximum(reach2, 1.0)
        return row + float(dy * rows), col + float(dx * cols), reach2, rate, tails[k, slot, 1:2, :]

    def tabulate(k, slot):
        lanes = slice(slot * slots, (slot + 1) * slots)
        row, col, reach2, rate, scale = place(k, slot)
        dx = OFFSETS[slot][1]
        dlat = lax.broadcasted_iota(jnp.int32, (rows, slots), 0).astype(f32) - row
        dlat2 = dlat * dlat
        reach_lat[k, :, lanes] = reach2 - dlat2
        decay_lat[k, :, lanes] = jnp.exp(dlat2 * rate) * scale
        if dx == 0:
            dlon = lax.broadcasted_iota(jnp.int32, (cols, slots), 0).astype(f32) - col
            gap_ref, decay_ref, here = gap_mid, decay_mid, lanes
        else:
            first = 0 if dx < 0 else cols - REACH
            dlon = lax.broadcasted_iota(jnp.int32, (REACH, slots), 0).astype(f32) + float(first) - col
            gap_ref, decay_ref = gap_side, decay_side
            here = slice((slot - 3) * slots, (slot - 2) * slots)
        dlon2 = dlon * dlon
        gap_ref[k, :, here] = dlon2
        decay_ref[k, :, here] = jnp.exp(dlon2 * rate)

    def update(k, q, group, parts, centring):
        cells = pl.ds(pl.multiple_of(q * chunk_cells + group * block, block), block)
        lat_rows = pl.ds(pl.multiple_of(group * GROUP, GROUP), GROUP)
        total = xt[cells, :]
        for first_slot, n_slots, side in parts:
            lanes = slice(first_slot * slots, (first_slot + n_slots) * slots)
            cov = jnp.dot(cent[cells, :], hp_all[k, :, lanes], preferred_element_type=f32)
            if side:
                here = slice((first_slot - 3) * slots, (first_slot - 3 + n_slots) * slots)
                gap, decay = gap_side[k, :, here], decay_side[k, :, here]
            else:
                columns = pl.ds(pl.multiple_of(q * REACH, REACH), REACH)
                gap, decay = gap_mid[k, columns, lanes], decay_mid[k, columns, lanes]
            reach = reach_lat[k, lat_rows, lanes]
            fade = decay_lat[k, lat_rows, lanes]
            pieces = []
            for r in range(GROUP):
                weight = jnp.where(gap <= reach[r : r + 1], decay * fade[r : r + 1], 0.0)
                pieces.append((cov[r * REACH : (r + 1) * REACH] * weight).astype(bf16))
            scaled = jnp.concatenate(pieces, axis=0)
            total += lax.dot_general(
                scaled, gain_all[k, :, lanes], (((1,), (1,)), ((), ())), preferred_element_type=f32
            )
        xt[cells, :] = total
        if centring:
            cent[cells, :] = total.astype(bf16)

    def sweep(k, first_q, n_q, parts, centring=False):
        def step(i):
            q = first_q + i // row_groups
            update(k, q, i % row_groups, parts, centring)

        repeat(n_q * row_groups, min(UNROLL, n_q * row_groups), step)

    def gather(k):
        chosen = order_s[k]

        def some(i, inner):
            for j in range(16):
                s = i * 16 + j
                hx[pl.ds(s, 1), :] = xt[pl.ds(spot_s[chosen, 0, 0, s], 1), :]
            return inner

        lax.fori_loop(0, slots // 16, some, 0)

    def aim(k):
        cell = jnp.broadcast_to(cell_ref[order_s[k], 0], (slots, slots))
        at_cell = jnp.transpose(cell.astype(f32)).astype(jnp.int32)
        row_at[...] = (at_cell >> COL_BITS).astype(f32)
        col_at[...] = (at_cell & (cols - 1)).astype(f32)
        hb[...] = hx[...].astype(bf16)

    def look(k, first_slot, n_slots):
        lanes = slice(first_slot * slots, (first_slot + n_slots) * slots)
        cov = jnp.dot(hb[...], hp_all[k, :, lanes], preferred_element_type=f32)
        parts = []
        for i in range(n_slots):
            row, col, reach2, rate, scale = place(k, first_slot + i)
            dlat = row_at[...] - row
            dlon = col_at[...] - col
            gap = dlat * dlat + dlon * dlon
            weight = jnp.where(gap <= reach2, jnp.exp(gap * rate) * scale, 0.0)
            parts.append((cov[:, i * slots : (i + 1) * slots] * weight).astype(bf16))
        scaled = jnp.concatenate(parts, axis=1)
        hx[...] += lax.dot_general(
            scaled, gain_all[k, :, lanes], (((1,), (1,)), ((), ())), preferred_element_type=f32
        )

    def prepare(k):
        chosen = order_s[k]
        prior = jnp.transpose(hx[...])
        pert = prior[:members]
        mean = prior[members : members + 1]
        var = jnp.sum(pert * pert, axis=0, keepdims=True) * (1.0 / (members - 1))
        error = error_ref[chosen, 0]
        total = var + error
        spread = 1.0 + jnp.sqrt(error / total)
        live = lax.broadcasted_iota(jnp.int32, (1, slots), 1) < count_s[0, 0, chosen]
        scale = jnp.where(live, -1.0 / (((members - 1) * total) * spread), 0.0)
        shift = jnp.where(live, (mean - value_ref[chosen, 0]) * spread, 0.0)
        code = cell_ref[chosen, 0] * RADIUS_SPAN + radius_ref[chosen, 0]
        packets[k, 0] = jnp.where(live, pert, 0.0).astype(bf16)
        tails[k, 0, 0:1, :] = shift
        tails[k, 0, 1:2, :] = scale
        tails[k, 0, 2:3, :] = code.astype(f32)

    def send(k):
        for group in SENDS:
            at(group, lambda slot: start(k, slot))

    def receive(k, slots_):
        at(slots_, lambda slot: wait_arrived(k, slot))
        for slot in slots_:
            unpack(k, slot)

    def finish(k):
        at(NEIGHBOURS, lambda slot: wait_sent(k, slot))

    def rest(k):
        for slot in NEIGHBOURS:
            tabulate(k, slot)
        sweep(k, 1, chunks - 2, (STACK,), centring=True)
        sweep(k, 0, 1, (STACK, (WEST, 3, True)), centring=True)
        sweep(k, chunks - 1, 1, (STACK, (EAST, 3, True)), centring=True)

    last = batches - 1

    def one_batch(k, carry):
        @pl.when(k > 0)
        def _():
            rest(k - 1)
            finish(k - 1)

        @pl.when(k < last)
        def _():
            gather(k + 1)
            aim(k + 1)

        unpack(k, 0)
        tabulate(k, 0)
        sweep(k, 0, chunks, ((0, 1, False),))

        @pl.when(k < last)
        def _():
            receive(k, (NORTH, SOUTH))
            look(k, 0, 3)
            receive(k, (WEST, EAST))
            look(k, WEST, 1)
            look(k, EAST, 1)
            receive(k, CORNERS)
            look(k, WEST + 1, 2)
            look(k, EAST + 1, 2)
            prepare(k + 1)
            send(k + 1)

        return carry

    spots.wait()
    gather(0)
    prepare(0)
    above = (lat + n_lat - 1) // n_lat
    below = (2 * n_lat - 2 - lat) // n_lat
    pl.semaphore_wait(barrier, 2 + 3 * above + 3 * below)
    send(0)
    lax.fori_loop(0, batches, one_batch, 0)

    receive(last, (NORTH, SOUTH))
    for slot in (NORTH, SOUTH):
        tabulate(last, slot)
    sweep(last, 0, chunks, (STACK,))
    receive(last, (WEST, EAST))
    for slot in (WEST, EAST):
        tabulate(last, slot)
    sweep(last, 0, 1, ((WEST, 1, True),))
    sweep(last, chunks - 1, 1, ((EAST, 1, True),))
    receive(last, CORNERS)
    for slot in CORNERS:
        tabulate(last, slot)
    sweep(last, 0, 1, ((WEST + 1, 2, True),))
    sweep(last, chunks - 1, 1, ((EAST + 1, 2, True),))

    def store_row(r):
        pieces = [
            xt[pl.ds(pl.multiple_of(q * chunk_cells + r * REACH, REACH), REACH), :]
            for q in range(chunks)
        ]
        v = jnp.transpose(jnp.concatenate(pieces, axis=0))
        out_ref[pl.ds(r, members, stride=rows), :] = v[:members] + v[members : members + 1]

    repeat(rows, 8, store_row)

    finish(last)


def local(ensemble, obs_value, obs_error, obs_cell, obs_radius, obs_count, batch_order):
    members, levels, rows, cols = ensemble.shape
    batches = obs_cell.shape[0]
    slots = obs_cell.shape[-1]
    assert levels == 1 and cols == LANES and slots == LANES and rows == REACH
    n_lat, n_lon = lax.axis_size("lat"), lax.axis_size("lon")
    padded = -(-members // LANES) * LANES
    cells = rows * cols
    tiles = len(OFFSETS)
    vmem = pl.BlockSpec(memory_space=pltpu.VMEM)
    hbm = pl.BlockSpec(memory_space=pltpu.HBM)
    f32, bf16, i32 = jnp.float32, jnp.bfloat16, jnp.int32
    small = (batches, 1, 1, slots)
    out = pl.pallas_call(
        functools.partial(kernel, (members, rows, cols, slots, batches, n_lat, n_lon)),
        out_shape=pltpu.VMEM((members * rows, cols), f32),
        in_specs=[hbm] * 7,
        out_specs=vmem,
        scratch_shapes=[
            pltpu.VMEM((members * rows, cols), f32),
            pltpu.VMEM(small, f32),
            pltpu.VMEM(small, f32),
            pltpu.VMEM(small, i32),
            pltpu.VMEM(small, i32),
            pltpu.VMEM(small, i32),
            pltpu.SMEM(small, i32),
            pltpu.SMEM((1, 1, batches), i32),
            pltpu.SMEM((batches,), i32),
            pltpu.VMEM((cells, padded), f32),
            pltpu.VMEM((cells, padded), bf16),
            pltpu.VMEM((slots, padded), f32),
            pltpu.VMEM((slots, padded), bf16),
            pltpu.VMEM((slots, slots), f32),
            pltpu.VMEM((slots, slots), f32),
            pltpu.VMEM((batches, tiles, members, slots), bf16),
            pltpu.VMEM((batches, tiles, 8, slots), f32),
            pltpu.VMEM((batches, padded, tiles * slots), bf16),
            pltpu.VMEM((batches, padded, tiles * slots), bf16),
            pltpu.VMEM((batches, rows, tiles * slots), f32),
            pltpu.VMEM((batches, rows, tiles * slots), f32),
            pltpu.VMEM((batches, cols, 3 * slots), f32),
            pltpu.VMEM((batches, cols, 3 * slots), f32),
            pltpu.VMEM((batches, REACH, 6 * slots), f32),
            pltpu.VMEM((batches, REACH, 6 * slots), f32),
            pltpu.SemaphoreType.DMA((8,)),
            pltpu.SemaphoreType.DMA((batches, tiles)),
            pltpu.SemaphoreType.DMA((batches, tiles)),
            pltpu.SemaphoreType.DMA((batches, tiles)),
            pltpu.SemaphoreType.DMA((batches, tiles)),
        ],
        compiler_params=pltpu.CompilerParams(
            collective_id=0, has_side_effects=True, vmem_limit_bytes=58 * 1024 * 1024
        ),
    )(
        ensemble.reshape(members * rows, cols),
        obs_value,
        obs_error,
        obs_cell,
        obs_radius,
        jnp.transpose(obs_count, (1, 2, 0)),
        batch_order,
    )
    return out.reshape(ensemble.shape)


def solution(mesh):
    return jax.shard_map(
        local,
        mesh=mesh,
        in_specs=(
            P(None, None, "lat", "lon"),
            P(None, "lat", "lon", None),
            P(None, "lat", "lon", None),
            P(None, "lat", "lon", None),
            P(None, "lat", "lon", None),
            P(None, "lat", "lon"),
            P(),
        ),
        out_specs=P(None, None, "lat", "lon"),
        check_vma=False,
    )
```

```python
import functools

import jax
import jax.numpy as jnp
from jax import lax
from jax.experimental import pallas as pl
from jax.experimental.pallas import tpu as pltpu
from jax.sharding import PartitionSpec as P

REACH = 32
LANES = 128
COL_BITS = 7
REACH_BITS = 5
TAIL = 16
LINES = 3
RADIUS_BITS = 6
RADIUS_SPAN = 1 << RADIUS_BITS
UNROLL = 16
GROUP = 16

OFFSETS = ((0, 0), (-1, 0), (1, 0), (0, -1), (-1, -1), (1, -1), (0, 1), (-1, 1), (1, 1))
NORTH, SOUTH, WEST, EAST = 1, 2, 3, 6
STACK = (NORTH, 2, False)
CORNERS = (4, 5, 7, 8)
BUFFER = (0, 1, 2, 3, 5, 7, 4, 6, 8)
GROUPS = ((3, 6), (1,), (2,), (4, 7), (5, 8))
SENDS = ((WEST, EAST), (NORTH, SOUTH), CORNERS)
NEIGHBOURS = (WEST, EAST, NORTH, SOUTH) + CORNERS


def repeat(count, unroll, body):
    def step(i, carry):
        for j in range(unroll):
            body(i * unroll + j)
        return carry

    lax.fori_loop(0, count // unroll, step, 0)


def opposite(slot):
    dy, dx = OFFSETS[slot]
    return OFFSETS.index((-dy, -dx))


def kernel(
    dims,
    x_hbm,
    value_hbm,
    error_hbm,
    cell_hbm,
    radius_hbm,
    count_hbm,
    order_hbm,
    out_ref,
    x_ref,
    value_ref,
    error_ref,
    cell_ref,
    radius_ref,
    spot_v,
    spot_s,
    count_s,
    order_s,
    xt,
    cent,
    hx,
    hb,
    row_at,
    col_at,
    packets,
    tails,
    hp_all,
    gain_all,
    reach_lat,
    decay_lat,
    gap_mid,
    decay_mid,
    gap_side,
    decay_side,
    copy_sem,
    send_sem,
    recv_sem,
    tail_send_sem,
    tail_recv_sem,
):
    members, rows, cols, slots, batches, n_lat, n_lon = dims
    padded = xt.shape[1]
    chunks = cols // REACH
    chunk_cells = rows * REACH
    row_groups = rows // GROUP
    block = GROUP * REACH
    f32, bf16 = jnp.float32, jnp.bfloat16
    lat = lax.axis_index("lat")
    lon = lax.axis_index("lon")
    has_north = lat > 0
    has_south = lat < n_lat - 1

    def device(slot):
        dy, dx = OFFSETS[slot]
        return (lat + dy, lax.rem(lon + dx + n_lon, n_lon))

    def at(slots_, action):
        for sign, present in ((0, None), (-1, has_north), (1, has_south)):
            chosen = [slot for slot in slots_ if OFFSETS[slot][0] == sign]
            if not chosen:
                continue
            if present is None:
                for slot in chosen:
                    action(slot)
            else:

                @pl.when(present)
                def _():
                    for slot in chosen:
                        action(slot)

    barrier = pltpu.get_barrier_semaphore()

    def greet(slot):
        pl.semaphore_signal(
            barrier, inc=1, device_id=device(slot), device_id_type=pl.DeviceIdType.MESH
        )

    at(NEIGHBOURS, greet)

    loads = [
        pltpu.make_async_copy(source, target, copy_sem.at[i])
        for i, (source, target) in enumerate(
            (
                (x_hbm, x_ref),
                (order_hbm, order_s),
                (count_hbm, count_s),
                (value_hbm, value_ref),
                (error_hbm, error_ref),
                (cell_hbm, cell_ref),
                (radius_hbm, radius_ref),
            )
        )
    ]
    for load in loads:
        load.start()

    for sign, present in ((-1, has_north), (1, has_south)):

        @pl.when(jnp.logical_not(present))
        def _():
            for slot in NEIGHBOURS:
                if OFFSETS[slot][0] == sign:
                    packets[:, BUFFER[slot]] = jnp.zeros((batches,) + packets.shape[2:], bf16)
                    tails[:, BUFFER[slot]] = jnp.zeros((batches,) + tails.shape[2:], f32)

    hp_all[:, members:] = jnp.zeros((batches, padded - members, hp_all.shape[2]), bf16)
    gain_all[:, members:] = jnp.zeros((batches, padded - members, gain_all.shape[2]), bf16)
    for load in loads:
        load.wait()
    cell = cell_ref[...]
    chunk = (cell & (cols - 1)) >> REACH_BITS
    spot_v[...] = chunk * chunk_cells + (cell >> COL_BITS) * REACH + (cell & (REACH - 1))
    spots = pltpu.make_async_copy(spot_v, spot_s, copy_sem.at[7])
    spots.start()

    def load_row(r):
        v = x_ref[pl.ds(r, members, stride=rows), :]
        mean = jnp.sum(v, axis=0, keepdims=True) * (1.0 / members)
        filler = jnp.where(
            lax.broadcasted_iota(jnp.int32, (padded - members, cols), 0) == 0, mean, 0.0
        )
        vt = jnp.transpose(jnp.concatenate([v - mean, filler], axis=0))
        vc = vt.astype(bf16)
        for q in range(chunks):
            start = pl.multiple_of(q * chunk_cells + r * REACH, REACH)
            xt[pl.ds(start, REACH), :] = vt[q * REACH : (q + 1) * REACH]
            cent[pl.ds(start, REACH), :] = vc[q * REACH : (q + 1) * REACH]

    repeat(rows, 8, load_row)

    def group_of(slot):
        return [slot in group for group in GROUPS].index(True)

    def moves(k, source, target, count, sender, receiver, toward):
        lines = pl.ds(0, LINES)
        here, there = pl.ds(source, count), pl.ds(target, count)
        return (
            pltpu.make_async_remote_copy(
                src_ref=packets.at[k, here],
                dst_ref=packets.at[k, there],
                send_sem=send_sem.at[k, sender + 1],
                recv_sem=recv_sem.at[k, receiver],
                device_id=device(toward),
                device_id_type=pl.DeviceIdType.MESH,
            ),
            pltpu.make_async_remote_copy(
                src_ref=tails.at[k, here, lines],
                dst_ref=tails.at[k, there, lines],
                send_sem=tail_send_sem.at[k, sender + 1],
                recv_sem=tail_recv_sem.at[k, receiver],
                device_id=device(toward),
                device_id_type=pl.DeviceIdType.MESH,
            ),
        )

    def start(k, slot):
        other = opposite(slot)
        for move in moves(k, 0, BUFFER[other], 1, OFFSETS[slot][0], group_of(other), slot):
            move.start()

    def wait_sent(k, slot):
        count = sum(OFFSETS[other][0] == OFFSETS[slot][0] for other in NEIGHBOURS)
        for move in moves(k, 0, 0, count, OFFSETS[slot][0], 0, EAST):
            move.wait_send()

    def wait_arrived(k, slot):
        group = group_of(slot)
        first = BUFFER[slot]
        for move in moves(k, first, first, len(GROUPS[group]), 0, group, EAST):
            move.wait_recv()

    def unpack(k, slot):
        lanes = slice(slot * slots, (slot + 1) * slots)
        hp = packets[k, BUFFER[slot]]
        hp_all[k, :members, lanes] = hp
        gain_all[k, :members, lanes] = hp
        first_row = lax.broadcasted_iota(jnp.int32, (TAIL, slots), 0) == 0
        shift = jnp.broadcast_to(tails[k, BUFFER[slot], 0:1, :], (TAIL, slots))
        gain_all[k, members : members + TAIL, lanes] = jnp.where(first_row, shift, 0.0).astype(bf16)

    def place(k, slot):
        dy, dx = OFFSETS[slot]
        code = tails[k, BUFFER[slot], 2:3, :].astype(jnp.int32)
        radius = (code & (RADIUS_SPAN - 1)).astype(f32)
        row = (code >> (RADIUS_BITS + COL_BITS)).astype(f32)
        col = ((code >> RADIUS_BITS) & (cols - 1)).astype(f32)
        reach2 = radius * radius
        rate = -2.0 / jnp.maximum(reach2, 1.0)
        return row + float(dy * rows), col + float(dx * cols), reach2, rate, tails[k, BUFFER[slot], 1:2, :]

    def tabulate(k, slot):
        lanes = slice(slot * slots, (slot + 1) * slots)
        row, col, reach2, rate, scale = place(k, slot)
        dx = OFFSETS[slot][1]
        dlat = lax.broadcasted_iota(jnp.int32, (rows, slots), 0).astype(f32) - row
        dlat2 = dlat * dlat
        reach_lat[k, :, lanes] = reach2 - dlat2
        decay_lat[k, :, lanes] = jnp.exp(dlat2 * rate) * scale
        if dx == 0:
            dlon = lax.broadcasted_iota(jnp.int32, (cols, slots), 0).astype(f32) - col
            gap_ref, decay_ref, here = gap_mid, decay_mid, lanes
        else:
            first = 0 if dx < 0 else cols - REACH
            dlon = lax.broadcasted_iota(jnp.int32, (REACH, slots), 0).astype(f32) + float(first) - col
            gap_ref, decay_ref = gap_side, decay_side
            here = slice((slot - 3) * slots, (slot - 2) * slots)
        dlon2 = dlon * dlon
        gap_ref[k, :, here] = dlon2
        decay_ref[k, :, here] = jnp.exp(dlon2 * rate)

    def update(k, q, group, parts, centring):
        cells = pl.ds(pl.multiple_of(q * chunk_cells + group * block, block), block)
        lat_rows = pl.ds(pl.multiple_of(group * GROUP, GROUP), GROUP)
        total = xt[cells, :]
        for first_slot, n_slots, side in parts:
            lanes = slice(first_slot * slots, (first_slot + n_slots) * slots)
            cov = jnp.dot(cent[cells, :], hp_all[k, :, lanes], preferred_element_type=f32)
            if side:
                here = slice((first_slot - 3) * slots, (first_slot - 3 + n_slots) * slots)
                gap, decay = gap_side[k, :, here], decay_side[k, :, here]
            else:
                columns = pl.ds(pl.multiple_of(q * REACH, REACH), REACH)
                gap, decay = gap_mid[k, columns, lanes], decay_mid[k, columns, lanes]
            reach = reach_lat[k, lat_rows, lanes]
            fade = decay_lat[k, lat_rows, lanes]
            pieces = []
            for r in range(GROUP):
                weight = jnp.where(gap <= reach[r : r + 1], decay * fade[r : r + 1], 0.0)
                pieces.append((cov[r * REACH : (r + 1) * REACH] * weight).astype(bf16))
            scaled = jnp.concatenate(pieces, axis=0)
            total += lax.dot_general(
                scaled, gain_all[k, :, lanes], (((1,), (1,)), ((), ())), preferred_element_type=f32
            )
        xt[cells, :] = total
        if centring:
            cent[cells, :] = total.astype(bf16)

    def sweep(k, first_q, n_q, parts, centring=False):
        def step(i):
            q = first_q + i // row_groups
            update(k, q, i % row_groups, parts, centring)

        repeat(n_q * row_groups, min(UNROLL, n_q * row_groups), step)

    def gather(k):
        chosen = order_s[k]

        def some(i, inner):
            for j in range(16):
                s = i * 16 + j
                hx[pl.ds(s, 1), :] = xt[pl.ds(spot_s[chosen, 0, 0, s], 1), :]
            return inner

        lax.fori_loop(0, slots // 16, some, 0)

    def aim(k):
        cell = jnp.broadcast_to(cell_ref[order_s[k], 0], (slots, slots))
        at_cell = jnp.transpose(cell.astype(f32)).astype(jnp.int32)
        row_at[...] = (at_cell >> COL_BITS).astype(f32)
        col_at[...] = (at_cell & (cols - 1)).astype(f32)
        hb[...] = hx[...].astype(bf16)

    def look(k, first_slot, n_slots):
        lanes = slice(first_slot * slots, (first_slot + n_slots) * slots)
        cov = jnp.dot(hb[...], hp_all[k, :, lanes], preferred_element_type=f32)
        parts = []
        for i in range(n_slots):
            row, col, reach2, rate, scale = place(k, first_slot + i)
            dlat = row_at[...] - row
            dlon = col_at[...] - col
            gap = dlat * dlat + dlon * dlon
            weight = jnp.where(gap <= reach2, jnp.exp(gap * rate) * scale, 0.0)
            parts.append((cov[:, i * slots : (i + 1) * slots] * weight).astype(bf16))
        scaled = jnp.concatenate(parts, axis=1)
        hx[...] += lax.dot_general(
            scaled, gain_all[k, :, lanes], (((1,), (1,)), ((), ())), preferred_element_type=f32
        )

    def prepare(k):
        chosen = order_s[k]
        prior = jnp.transpose(hx[...])
        pert = prior[:members]
        mean = prior[members : members + 1]
        var = jnp.sum(pert * pert, axis=0, keepdims=True) * (1.0 / (members - 1))
        error = error_ref[chosen, 0]
        total = var + error
        spread = 1.0 + jnp.sqrt(error / total)
        live = lax.broadcasted_iota(jnp.int32, (1, slots), 1) < count_s[0, 0, chosen]
        scale = jnp.where(live, -1.0 / (((members - 1) * total) * spread), 0.0)
        shift = jnp.where(live, (mean - value_ref[chosen, 0]) * spread, 0.0)
        code = cell_ref[chosen, 0] * RADIUS_SPAN + radius_ref[chosen, 0]
        packets[k, 0] = jnp.where(live, pert, 0.0).astype(bf16)
        tails[k, 0, 0:1, :] = shift
        tails[k, 0, 1:2, :] = scale
        tails[k, 0, 2:3, :] = code.astype(f32)

    def send(k):
        for group in SENDS:
            at(group, lambda slot: start(k, slot))

    def receive(k, slots_):
        at([slot for slot in slots_ if OFFSETS[slot][1] <= 0], lambda slot: wait_arrived(k, slot))
        for slot in slots_:
            unpack(k, slot)

    def finish(k):
        at((WEST, NORTH, SOUTH), lambda slot: wait_sent(k, slot))

    def rest(k):
        for slot in NEIGHBOURS:
            tabulate(k, slot)
        sweep(k, 1, chunks - 2, (STACK,), centring=True)
        sweep(k, 0, 1, (STACK, (WEST, 3, True)), centring=True)
        sweep(k, chunks - 1, 1, (STACK, (EAST, 3, True)), centring=True)

    last = batches - 1

    def one_batch(k, carry):
        @pl.when(k > 0)
        def _():
            rest(k - 1)
            finish(k - 1)

        @pl.when(k < last)
        def _():
            gather(k + 1)
            aim(k + 1)

        unpack(k, 0)
        tabulate(k, 0)
        sweep(k, 0, chunks, ((0, 1, False),))

        @pl.when(k < last)
        def _():
            receive(k, (NORTH, SOUTH))
            look(k, 0, 3)
            receive(k, (WEST, EAST))
            look(k, WEST, 1)
            look(k, EAST, 1)
            receive(k, CORNERS)
            look(k, WEST + 1, 2)
            look(k, EAST + 1, 2)
            prepare(k + 1)
            send(k + 1)

        return carry

    spots.wait()
    gather(0)
    prepare(0)
    above = (lat + n_lat - 1) // n_lat
    below = (2 * n_lat - 2 - lat) // n_lat
    pl.semaphore_wait(barrier, 2 + 3 * above + 3 * below)
    send(0)
    lax.fori_loop(0, batches, one_batch, 0)

    receive(last, (NORTH, SOUTH))
    for slot in (NORTH, SOUTH):
        tabulate(last, slot)
    sweep(last, 0, chunks, (STACK,))
    receive(last, (WEST, EAST))
    for slot in (WEST, EAST):
        tabulate(last, slot)
    sweep(last, 0, 1, ((WEST, 1, True),))
    sweep(last, chunks - 1, 1, ((EAST, 1, True),))
    receive(last, CORNERS)
    for slot in CORNERS:
        tabulate(last, slot)
    sweep(last, 0, 1, ((WEST + 1, 2, True),))
    sweep(last, chunks - 1, 1, ((EAST + 1, 2, True),))

    def store_rows(g):
        lines = []
        for r in range(8):
            pieces = [
                xt[pl.ds(pl.multiple_of(q * chunk_cells + (g * 8 + r) * REACH, REACH), REACH), :]
                for q in range(chunks)
            ]
            v = jnp.transpose(jnp.concatenate(pieces, axis=0))
            lines.append((v[:members] + v[members : members + 1])[None])
        v = jnp.swapaxes(jnp.concatenate(lines, axis=0), 0, 1)
        out_ref[:, pl.ds(pl.multiple_of(g * 8, 8), 8), :] = v

    repeat(rows // 8, 1, store_rows)

    finish(last)


def local(ensemble, obs_value, obs_error, obs_cell, obs_radius, obs_count, batch_order):
    members, levels, rows, cols = ensemble.shape
    batches = obs_cell.shape[0]
    slots = obs_cell.shape[-1]
    assert levels == 1 and cols == LANES and slots == LANES and rows == REACH
    n_lat, n_lon = lax.axis_size("lat"), lax.axis_size("lon")
    padded = -(-members // LANES) * LANES
    cells = rows * cols
    tiles = len(OFFSETS)
    vmem = pl.BlockSpec(memory_space=pltpu.VMEM)
    hbm = pl.BlockSpec(memory_space=pltpu.HBM)
    f32, bf16, i32 = jnp.float32, jnp.bfloat16, jnp.int32
    small = (batches, 1, 1, slots)
    out = pl.pallas_call(
        functools.partial(kernel, (members, rows, cols, slots, batches, n_lat, n_lon)),
        out_shape=pltpu.VMEM((members, rows, cols), f32),
        in_specs=[hbm] * 7,
        out_specs=vmem,
        scratch_shapes=[
            pltpu.VMEM((members * rows, cols), f32),
            pltpu.VMEM(small, f32),
            pltpu.VMEM(small, f32),
            pltpu.VMEM(small, i32),
            pltpu.VMEM(small, i32),
            pltpu.VMEM(small, i32),
            pltpu.SMEM(small, i32),
            pltpu.SMEM((1, 1, batches), i32),
            pltpu.SMEM((batches,), i32),
            pltpu.VMEM((cells, padded), f32),
            pltpu.VMEM((cells, padded), bf16),
            pltpu.VMEM((slots, padded), f32),
            pltpu.VMEM((slots, padded), bf16),
            pltpu.VMEM((slots, slots), f32),
            pltpu.VMEM((slots, slots), f32),
            pltpu.VMEM((batches, tiles, members, slots), bf16),
            pltpu.VMEM((batches, tiles, 8, slots), f32),
            pltpu.VMEM((batches, padded, tiles * slots), bf16),
            pltpu.VMEM((batches, padded, tiles * slots), bf16),
            pltpu.VMEM((batches, rows, tiles * slots), f32),
            pltpu.VMEM((batches, rows, tiles * slots), f32),
            pltpu.VMEM((batches, cols, 3 * slots), f32),
            pltpu.VMEM((batches, cols, 3 * slots), f32),
            pltpu.VMEM((batches, REACH, 6 * slots), f32),
            pltpu.VMEM((batches, REACH, 6 * slots), f32),
            pltpu.SemaphoreType.DMA((8,)),
            pltpu.SemaphoreType.DMA((batches, 3)),
            pltpu.SemaphoreType.DMA((batches, len(GROUPS))),
            pltpu.SemaphoreType.DMA((batches, 3)),
            pltpu.SemaphoreType.DMA((batches, len(GROUPS))),
        ],
        compiler_params=pltpu.CompilerParams(
            collective_id=0, has_side_effects=True, vmem_limit_bytes=58 * 1024 * 1024
        ),
    )(
        ensemble.reshape(members * rows, cols),
        obs_value,
        obs_error,
        obs_cell,
        obs_radius,
        jnp.transpose(obs_count, (1, 2, 0)),
        batch_order,
    )
    return out.reshape(ensemble.shape)


def solution(mesh):
    return jax.shard_map(
        local,
        mesh=mesh,
        in_specs=(
            P(None, None, "lat", "lon"),
            P(None, "lat", "lon", None),
            P(None, "lat", "lon", None),
            P(None, "lat", "lon", None),
            P(None, "lat", "lon", None),
            P(None, "lat", "lon"),
            P(),
        ),
        out_specs=P(None, None, "lat", "lon"),
        check_vma=False,
    )
```

```python
import functools

import jax
import jax.numpy as jnp
from jax import lax
from jax.experimental import pallas as pl
from jax.experimental.pallas import tpu as pltpu
from jax.sharding import PartitionSpec as P

REACH = 32
LANES = 128
COL_BITS = 7
REACH_BITS = 5
TAIL = 16
LINES = 3
RADIUS_BITS = 6
RADIUS_SPAN = 1 << RADIUS_BITS
UNROLL = 16
GROUP = 16

OFFSETS = ((0, 0), (-1, 0), (1, 0), (0, -1), (-1, -1), (1, -1), (0, 1), (-1, 1), (1, 1))
NORTH, SOUTH, WEST, EAST = 1, 2, 3, 6
STACK = (NORTH, 2, False)
CORNERS = (4, 5, 7, 8)
BUFFER = (0, 1, 2, 3, 5, 7, 4, 6, 8)
GROUPS = ((3, 6), (1,), (2,), (4, 7), (5, 8))
SENDS = ((WEST, EAST), (NORTH, SOUTH), CORNERS)
NEIGHBOURS = (WEST, EAST, NORTH, SOUTH) + CORNERS


def repeat(count, unroll, body):
    def step(i, carry):
        for j in range(unroll):
            body(i * unroll + j)
        return carry

    lax.fori_loop(0, count // unroll, step, 0)


def opposite(slot):
    dy, dx = OFFSETS[slot]
    return OFFSETS.index((-dy, -dx))


def kernel(
    dims,
    x_hbm,
    value_hbm,
    error_hbm,
    cell_hbm,
    radius_hbm,
    count_hbm,
    order_hbm,
    out_ref,
    x_ref,
    value_ref,
    error_ref,
    cell_ref,
    radius_ref,
    spot_v,
    spot_s,
    count_s,
    order_s,
    xt,
    cent,
    hx,
    hb,
    row_at,
    col_at,
    packets,
    tails,
    hp_all,
    gain_all,
    reach_lat,
    decay_lat,
    gap_mid,
    decay_mid,
    gap_side,
    decay_side,
    copy_sem,
    send_sem,
    recv_sem,
    tail_send_sem,
    tail_recv_sem,
):
    members, rows, cols, slots, batches, n_lat, n_lon = dims
    padded = xt.shape[1]
    chunks = cols // REACH
    chunk_cells = rows * REACH
    row_groups = rows // GROUP
    block = GROUP * REACH
    f32, bf16 = jnp.float32, jnp.bfloat16
    lat = lax.axis_index("lat")
    lon = lax.axis_index("lon")
    has_north = lat > 0
    has_south = lat < n_lat - 1

    def device(slot):
        dy, dx = OFFSETS[slot]
        return (lat + dy, lax.rem(lon + dx + n_lon, n_lon))

    def at(slots_, action):
        for sign, present in ((0, None), (-1, has_north), (1, has_south)):
            chosen = [slot for slot in slots_ if OFFSETS[slot][0] == sign]
            if not chosen:
                continue
            if present is None:
                for slot in chosen:
                    action(slot)
            else:

                @pl.when(present)
                def _():
                    for slot in chosen:
                        action(slot)

    barrier = pltpu.get_barrier_semaphore()

    def greet(slot):
        pl.semaphore_signal(
            barrier, inc=1, device_id=device(slot), device_id_type=pl.DeviceIdType.MESH
        )

    at(NEIGHBOURS, greet)

    loads = [
        pltpu.make_async_copy(source, target, copy_sem.at[i])
        for i, (source, target) in enumerate(
            (
                (x_hbm, x_ref),
                (order_hbm, order_s),
                (count_hbm, count_s),
                (value_hbm, value_ref),
                (error_hbm, error_ref),
                (cell_hbm, cell_ref),
                (radius_hbm, radius_ref),
            )
        )
    ]
    for load in loads:
        load.start()

    for sign, present in ((-1, has_north), (1, has_south)):

        @pl.when(jnp.logical_not(present))
        def _():
            for slot in NEIGHBOURS:
                if OFFSETS[slot][0] == sign:
                    packets[:, BUFFER[slot]] = jnp.zeros((batches,) + packets.shape[2:], bf16)
                    tails[:, BUFFER[slot]] = jnp.zeros((batches,) + tails.shape[2:], f32)

    hp_all[:, members:] = jnp.zeros((batches, padded - members, hp_all.shape[2]), bf16)
    gain_all[:, members:] = jnp.zeros((batches, padded - members, gain_all.shape[2]), bf16)
    for load in loads:
        load.wait()
    cell = cell_ref[...]
    chunk = (cell & (cols - 1)) >> REACH_BITS
    spot_v[...] = chunk * chunk_cells + (cell >> COL_BITS) * REACH + (cell & (REACH - 1))
    spots = pltpu.make_async_copy(spot_v, spot_s, copy_sem.at[7])
    spots.start()

    def load_row(r):
        v = x_ref[pl.ds(r, members, stride=rows), :]
        mean = jnp.sum(v, axis=0, keepdims=True) * (1.0 / members)
        filler = jnp.where(
            lax.broadcasted_iota(jnp.int32, (padded - members, cols), 0) == 0, mean, 0.0
        )
        vt = jnp.transpose(jnp.concatenate([v - mean, filler], axis=0))
        vc = vt.astype(bf16)
        for q in range(chunks):
            start = pl.multiple_of(q * chunk_cells + r * REACH, REACH)
            xt[pl.ds(start, REACH), :] = vt[q * REACH : (q + 1) * REACH]
            cent[pl.ds(start, REACH), :] = vc[q * REACH : (q + 1) * REACH]

    repeat(rows, 8, load_row)

    def group_of(slot):
        return [slot in group for group in GROUPS].index(True)

    def moves(k, source, target, count, sender, receiver, toward):
        lines = pl.ds(0, LINES)
        here, there = pl.ds(source, count), pl.ds(target, count)
        return (
            pltpu.make_async_remote_copy(
                src_ref=packets.at[k, here],
                dst_ref=packets.at[k, there],
                send_sem=send_sem.at[k, sender + 1],
                recv_sem=recv_sem.at[k, receiver],
                device_id=device(toward),
                device_id_type=pl.DeviceIdType.MESH,
            ),
            pltpu.make_async_remote_copy(
                src_ref=tails.at[k, here, lines],
                dst_ref=tails.at[k, there, lines],
                send_sem=tail_send_sem.at[k, sender + 1],
                recv_sem=tail_recv_sem.at[k, receiver],
                device_id=device(toward),
                device_id_type=pl.DeviceIdType.MESH,
            ),
        )

    def start(k, slot):
        other = opposite(slot)
        for move in moves(k, 0, BUFFER[other], 1, OFFSETS[slot][0], group_of(other), slot):
            move.start()

    def wait_sent(k, slot):
        count = sum(OFFSETS[other][0] == OFFSETS[slot][0] for other in NEIGHBOURS)
        for move in moves(k, 0, 0, count, OFFSETS[slot][0], 0, EAST):
            move.wait_send()

    def wait_arrived(k, slot):
        group = group_of(slot)
        first = BUFFER[slot]
        for move in moves(k, first, first, len(GROUPS[group]), 0, group, EAST):
            move.wait_recv()

    def unpack(k, slot):
        lanes = slice(slot * slots, (slot + 1) * slots)
        hp = packets[k, BUFFER[slot]]
        hp_all[k, :members, lanes] = hp
        gain_all[k, :members, lanes] = hp
        first_row = lax.broadcasted_iota(jnp.int32, (TAIL, slots), 0) == 0
        shift = jnp.broadcast_to(tails[k, BUFFER[slot], 0:1, :], (TAIL, slots))
        gain_all[k, members : members + TAIL, lanes] = jnp.where(first_row, shift, 0.0).astype(bf16)

    def place(k, slot):
        dy, dx = OFFSETS[slot]
        code = tails[k, BUFFER[slot], 2:3, :].astype(jnp.int32)
        radius = (code & (RADIUS_SPAN - 1)).astype(f32)
        row = (code >> (RADIUS_BITS + COL_BITS)).astype(f32)
        col = ((code >> RADIUS_BITS) & (cols - 1)).astype(f32)
        reach2 = radius * radius
        rate = -2.0 / jnp.maximum(reach2, 1.0)
        return row + float(dy * rows), col + float(dx * cols), reach2, rate, tails[k, BUFFER[slot], 1:2, :]

    def tabulate(k, slot):
        lanes = slice(slot * slots, (slot + 1) * slots)
        row, col, reach2, rate, scale = place(k, slot)
        dx = OFFSETS[slot][1]
        dlat = lax.broadcasted_iota(jnp.int32, (rows, slots), 0).astype(f32) - row
        dlat2 = dlat * dlat
        reach_lat[k, :, lanes] = reach2 - dlat2
        decay_lat[k, :, lanes] = jnp.exp(dlat2 * rate) * scale
        if dx == 0:
            dlon = lax.broadcasted_iota(jnp.int32, (cols, slots), 0).astype(f32) - col
            gap_ref, decay_ref, here = gap_mid, decay_mid, lanes
        else:
            first = 0 if dx < 0 else cols - REACH
            dlon = lax.broadcasted_iota(jnp.int32, (REACH, slots), 0).astype(f32) + float(first) - col
            gap_ref, decay_ref = gap_side, decay_side
            here = slice((slot - 3) * slots, (slot - 2) * slots)
        dlon2 = dlon * dlon
        gap_ref[k, :, here] = dlon2
        decay_ref[k, :, here] = jnp.exp(dlon2 * rate)

    def update(k, q, group, parts, centring):
        cells = pl.ds(pl.multiple_of(q * chunk_cells + group * block, block), block)
        lat_rows = pl.ds(pl.multiple_of(group * GROUP, GROUP), GROUP)
        total = xt[cells, :]
        for first_slot, n_slots, side in parts:
            lanes = slice(first_slot * slots, (first_slot + n_slots) * slots)
            cov = jnp.dot(cent[cells, :], hp_all[k, :, lanes], preferred_element_type=f32)
            if side:
                here = slice((first_slot - 3) * slots, (first_slot - 3 + n_slots) * slots)
                gap, decay = gap_side[k, :, here], decay_side[k, :, here]
            else:
                columns = pl.ds(pl.multiple_of(q * REACH, REACH), REACH)
                gap, decay = gap_mid[k, columns, lanes], decay_mid[k, columns, lanes]
            reach = reach_lat[k, lat_rows, lanes]
            fade = decay_lat[k, lat_rows, lanes]
            pieces = []
            for r in range(GROUP):
                weight = jnp.where(gap <= reach[r : r + 1], decay * fade[r : r + 1], 0.0)
                pieces.append((cov[r * REACH : (r + 1) * REACH] * weight).astype(bf16))
            scaled = jnp.concatenate(pieces, axis=0)
            total += lax.dot_general(
                scaled, gain_all[k, :, lanes], (((1,), (1,)), ((), ())), preferred_element_type=f32
            )
        xt[cells, :] = total
        if centring:
            cent[cells, :] = total.astype(bf16)

    def sweep(k, first_q, n_q, parts, centring=False):
        def step(i):
            q = first_q + i // row_groups
            update(k, q, i % row_groups, parts, centring)

        repeat(n_q * row_groups, min(UNROLL, n_q * row_groups), step)

    def gather(k):
        chosen = order_s[k]

        for s in range(slots):
            hx[pl.ds(s, 1), :] = xt[pl.ds(spot_s[chosen, 0, 0, s], 1), :]

    def aim(k):
        cell = jnp.broadcast_to(cell_ref[order_s[k], 0], (slots, slots))
        at_cell = jnp.transpose(cell.astype(f32)).astype(jnp.int32)
        row_at[...] = (at_cell >> COL_BITS).astype(f32)
        col_at[...] = (at_cell & (cols - 1)).astype(f32)
        hb[...] = hx[...].astype(bf16)

    def look(k, first_slot, n_slots):
        lanes = slice(first_slot * slots, (first_slot + n_slots) * slots)
        cov = jnp.dot(hb[...], hp_all[k, :, lanes], preferred_element_type=f32)
        parts = []
        for i in range(n_slots):
            row, col, reach2, rate, scale = place(k, first_slot + i)
            dlat = row_at[...] - row
            dlon = col_at[...] - col
            gap = dlat * dlat + dlon * dlon
            weight = jnp.where(gap <= reach2, jnp.exp(gap * rate) * scale, 0.0)
            parts.append((cov[:, i * slots : (i + 1) * slots] * weight).astype(bf16))
        scaled = jnp.concatenate(parts, axis=1)
        hx[...] += lax.dot_general(
            scaled, gain_all[k, :, lanes], (((1,), (1,)), ((), ())), preferred_element_type=f32
        )

    def prepare(k):
        chosen = order_s[k]
        prior = jnp.transpose(hx[...])
        pert = prior[:members]
        mean = prior[members : members + 1]
        var = jnp.sum(pert * pert, axis=0, keepdims=True) * (1.0 / (members - 1))
        error = error_ref[chosen, 0]
        total = var + error
        spread = 1.0 + jnp.sqrt(error / total)
        live = lax.broadcasted_iota(jnp.int32, (1, slots), 1) < count_s[0, 0, chosen]
        scale = jnp.where(live, -1.0 / (((members - 1) * total) * spread), 0.0)
        shift = jnp.where(live, (mean - value_ref[chosen, 0]) * spread, 0.0)
        code = cell_ref[chosen, 0] * RADIUS_SPAN + radius_ref[chosen, 0]
        packets[k, 0] = jnp.where(live, pert, 0.0).astype(bf16)
        tails[k, 0, 0:1, :] = shift
        tails[k, 0, 1:2, :] = scale
        tails[k, 0, 2:3, :] = code.astype(f32)

    def send(k):
        for group in SENDS:
            at(group, lambda slot: start(k, slot))

    def receive(k, slots_):
        at([slot for slot in slots_ if OFFSETS[slot][1] <= 0], lambda slot: wait_arrived(k, slot))
        for slot in slots_:
            unpack(k, slot)

    def finish(k):
        at((WEST, NORTH, SOUTH), lambda slot: wait_sent(k, slot))

    def rest(k):
        for slot in NEIGHBOURS:
            tabulate(k, slot)
        sweep(k, 1, chunks - 2, (STACK,), centring=True)
        sweep(k, 0, 1, (STACK, (WEST, 3, True)), centring=True)
        sweep(k, chunks - 1, 1, (STACK, (EAST, 3, True)), centring=True)

    last = batches - 1
    assert batches > 1

    def centre(k):
        unpack(k, 0)
        tabulate(k, 0)
        sweep(k, 0, chunks, ((0, 1, False),))

    def follow(k):
        receive(k, (NORTH, SOUTH, WEST, EAST))
        look(k, 1, 2)
        look(k, WEST, 1)
        look(k, EAST, 1)
        receive(k, CORNERS)
        look(k, WEST + 1, 2)
        look(k, EAST + 1, 2)
        prepare(k + 1)
        send(k + 1)

    def one_batch(k, carry):
        rest(k - 1)
        gather(k + 1)
        aim(k + 1)
        centre(k)
        look(k, 0, 1)
        finish(k - 1)
        follow(k)
        return carry

    spots.wait()
    gather(0)
    prepare(0)
    above = (lat + n_lat - 1) // n_lat
    below = (2 * n_lat - 2 - lat) // n_lat
    pl.semaphore_wait(barrier, 2 + 3 * above + 3 * below)
    send(0)
    gather(1)
    aim(1)
    centre(0)
    look(0, 0, 1)
    follow(0)
    lax.fori_loop(1, last, one_batch, 0)

    rest(last - 1)
    centre(last)
    finish(last - 1)
    receive(last, (NORTH,))
    tabulate(last, NORTH)
    sweep(last, 0, chunks, ((NORTH, 1, False),))
    receive(last, (WEST, EAST) + CORNERS[::2])
    for slot in (WEST, EAST) + CORNERS[::2]:
        tabulate(last, slot)
    sweep(last, 0, 1, ((WEST, 1, True), (CORNERS[::2][0], 1, True)))
    sweep(last, chunks - 1, 1, ((EAST, 1, True), (CORNERS[::2][1], 1, True)))
    receive(last, (SOUTH,) + CORNERS[1::2])
    for slot in (SOUTH,) + CORNERS[1::2]:
        tabulate(last, slot)
    sweep(last, 1, chunks - 2, ((SOUTH, 1, False),))
    sweep(last, 0, 1, ((SOUTH, 1, False), (CORNERS[1::2][0], 1, True)))
    sweep(last, chunks - 1, 1, ((SOUTH, 1, False), (CORNERS[1::2][1], 1, True)))

    def store_rows(g):
        lines = []
        for r in range(8):
            pieces = [
                xt[pl.ds(pl.multiple_of(q * chunk_cells + (g * 8 + r) * REACH, REACH), REACH), :]
                for q in range(chunks)
            ]
            v = jnp.transpose(jnp.concatenate(pieces, axis=0))
            lines.append((v[:members] + v[members : members + 1])[None])
        v = jnp.swapaxes(jnp.concatenate(lines, axis=0), 0, 1)
        out_ref[:, pl.ds(pl.multiple_of(g * 8, 8), 8), :] = v

    repeat(rows // 8, 1, store_rows)

    finish(last)


def local(ensemble, obs_value, obs_error, obs_cell, obs_radius, obs_count, batch_order):
    members, levels, rows, cols = ensemble.shape
    batches = obs_cell.shape[0]
    slots = obs_cell.shape[-1]
    assert levels == 1 and cols == LANES and slots == LANES and rows == REACH
    n_lat, n_lon = lax.axis_size("lat"), lax.axis_size("lon")
    padded = -(-members // LANES) * LANES
    cells = rows * cols
    tiles = len(OFFSETS)
    vmem = pl.BlockSpec(memory_space=pltpu.VMEM)
    hbm = pl.BlockSpec(memory_space=pltpu.HBM)
    f32, bf16, i32 = jnp.float32, jnp.bfloat16, jnp.int32
    small = (batches, 1, 1, slots)
    out = pl.pallas_call(
        functools.partial(kernel, (members, rows, cols, slots, batches, n_lat, n_lon)),
        out_shape=pltpu.VMEM((members, rows, cols), f32),
        in_specs=[hbm] * 7,
        out_specs=vmem,
        scratch_shapes=[
            pltpu.VMEM((members * rows, cols), f32),
            pltpu.VMEM(small, f32),
            pltpu.VMEM(small, f32),
            pltpu.VMEM(small, i32),
            pltpu.VMEM(small, i32),
            pltpu.VMEM(small, i32),
            pltpu.SMEM(small, i32),
            pltpu.SMEM((1, 1, batches), i32),
            pltpu.SMEM((batches,), i32),
            pltpu.VMEM((cells, padded), f32),
            pltpu.VMEM((cells, padded), bf16),
            pltpu.VMEM((slots, padded), f32),
            pltpu.VMEM((slots, padded), bf16),
            pltpu.VMEM((slots, slots), f32),
            pltpu.VMEM((slots, slots), f32),
            pltpu.VMEM((batches, tiles, members, slots), bf16),
            pltpu.VMEM((batches, tiles, 8, slots), f32),
            pltpu.VMEM((batches, padded, tiles * slots), bf16),
            pltpu.VMEM((batches, padded, tiles * slots), bf16),
            pltpu.VMEM((batches, rows, tiles * slots), f32),
            pltpu.VMEM((batches, rows, tiles * slots), f32),
            pltpu.VMEM((batches, cols, 3 * slots), f32),
            pltpu.VMEM((batches, cols, 3 * slots), f32),
            pltpu.VMEM((batches, REACH, 6 * slots), f32),
            pltpu.VMEM((batches, REACH, 6 * slots), f32),
            pltpu.SemaphoreType.DMA((8,)),
            pltpu.SemaphoreType.DMA((batches, 3)),
            pltpu.SemaphoreType.DMA((batches, len(GROUPS))),
            pltpu.SemaphoreType.DMA((batches, 3)),
            pltpu.SemaphoreType.DMA((batches, len(GROUPS))),
        ],
        compiler_params=pltpu.CompilerParams(
            collective_id=0, has_side_effects=True, vmem_limit_bytes=58 * 1024 * 1024
        ),
    )(
        ensemble.reshape(members * rows, cols),
        obs_value,
        obs_error,
        obs_cell,
        obs_radius,
        jnp.transpose(obs_count, (1, 2, 0)),
        batch_order,
    )
    return out.reshape(ensemble.shape)


def solution(mesh):
    return jax.shard_map(
        local,
        mesh=mesh,
        in_specs=(
            P(None, None, "lat", "lon"),
            P(None, "lat", "lon", None),
            P(None, "lat", "lon", None),
            P(None, "lat", "lon", None),
            P(None, "lat", "lon", None),
            P(None, "lat", "lon"),
            P(),
        ),
        out_specs=P(None, None, "lat", "lon"),
        check_vma=False,
    )
```

```python
import functools

import jax
import jax.numpy as jnp
from jax import lax
from jax.experimental import pallas as pl
from jax.experimental.pallas import tpu as pltpu
from jax.sharding import PartitionSpec as P

REACH = 32
LANES = 128
COL_BITS = 7
REACH_BITS = 5
TAIL = 16
LINES = 3
RADIUS_BITS = 6
RADIUS_SPAN = 1 << RADIUS_BITS
UNROLL = 16
GROUP = 16

OFFSETS = ((0, 0), (-1, 0), (1, 0), (0, -1), (-1, -1), (1, -1), (0, 1), (-1, 1), (1, 1))
NORTH, SOUTH, WEST, EAST = 1, 2, 3, 6
STACK = (NORTH, 2, False)
CORNERS = (4, 5, 7, 8)
BUFFER = (0, 1, 2, 3, 5, 7, 4, 6, 8)
GROUPS = ((3, 6), (1,), (2,), (4, 7), (5, 8))
SENDS = ((WEST, EAST), (NORTH, SOUTH), CORNERS)
NEIGHBOURS = (WEST, EAST, NORTH, SOUTH) + CORNERS


def repeat(count, unroll, body):
    def step(i, carry):
        for j in range(unroll):
            body(i * unroll + j)
        return carry

    lax.fori_loop(0, count // unroll, step, 0)


def opposite(slot):
    dy, dx = OFFSETS[slot]
    return OFFSETS.index((-dy, -dx))


def kernel(
    dims,
    x_hbm,
    value_hbm,
    error_hbm,
    cell_hbm,
    radius_hbm,
    count_hbm,
    order_hbm,
    out_ref,
    x_ref,
    value_ref,
    error_ref,
    cell_ref,
    radius_ref,
    spot_v,
    spot_s,
    count_s,
    order_s,
    xt,
    cent,
    hx,
    hb,
    row_at,
    col_at,
    turned,
    packets,
    tails,
    hp_all,
    gain_all,
    reach_lat,
    decay_lat,
    gap_mid,
    decay_mid,
    gap_side,
    decay_side,
    copy_sem,
    send_sem,
    recv_sem,
    tail_send_sem,
    tail_recv_sem,
):
    members, rows, cols, slots, batches, n_lat, n_lon = dims
    padded = xt.shape[1]
    chunks = cols // REACH
    chunk_cells = rows * REACH
    row_groups = rows // GROUP
    block = GROUP * REACH
    f32, bf16 = jnp.float32, jnp.bfloat16
    lat = lax.axis_index("lat")
    lon = lax.axis_index("lon")
    has_north = lat > 0
    has_south = lat < n_lat - 1

    def device(slot):
        dy, dx = OFFSETS[slot]
        return (lat + dy, lax.rem(lon + dx + n_lon, n_lon))

    def at(slots_, action):
        for sign, present in ((0, None), (-1, has_north), (1, has_south)):
            chosen = [slot for slot in slots_ if OFFSETS[slot][0] == sign]
            if not chosen:
                continue
            if present is None:
                for slot in chosen:
                    action(slot)
            else:

                @pl.when(present)
                def _():
                    for slot in chosen:
                        action(slot)

    barrier = pltpu.get_barrier_semaphore()

    def greet(slot):
        pl.semaphore_signal(
            barrier, inc=1, device_id=device(slot), device_id_type=pl.DeviceIdType.MESH
        )

    at(NEIGHBOURS, greet)

    loads = [
        pltpu.make_async_copy(source, target, copy_sem.at[i])
        for i, (source, target) in enumerate(
            (
                (x_hbm, x_ref),
                (order_hbm, order_s),
                (count_hbm, count_s),
                (value_hbm, value_ref),
                (error_hbm, error_ref),
                (cell_hbm, cell_ref),
                (radius_hbm, radius_ref),
            )
        )
    ]
    for load in loads:
        load.start()

    for sign, present in ((-1, has_north), (1, has_south)):

        @pl.when(jnp.logical_not(present))
        def _():
            for slot in NEIGHBOURS:
                if OFFSETS[slot][0] == sign:
                    packets[:, BUFFER[slot]] = jnp.zeros((batches,) + packets.shape[2:], bf16)
                    tails[:, BUFFER[slot]] = jnp.zeros((batches,) + tails.shape[2:], f32)

    hp_all[:, members:] = jnp.zeros((batches, padded - members, hp_all.shape[2]), bf16)
    gain_all[:, members:] = jnp.zeros((batches, padded - members, gain_all.shape[2]), bf16)
    for load in loads:
        load.wait()
    cell = cell_ref[...]
    chunk = (cell & (cols - 1)) >> REACH_BITS
    spot_v[...] = chunk * chunk_cells + (cell >> COL_BITS) * REACH + (cell & (REACH - 1))
    spots = pltpu.make_async_copy(spot_v, spot_s, copy_sem.at[7])
    spots.start()

    def load_row(r):
        v = x_ref[pl.ds(r, members, stride=rows), :]
        mean = jnp.sum(v, axis=0, keepdims=True) * (1.0 / members)
        filler = jnp.where(
            lax.broadcasted_iota(jnp.int32, (padded - members, cols), 0) == 0, mean, 0.0
        )
        vt = jnp.transpose(jnp.concatenate([v - mean, filler], axis=0))
        vc = vt.astype(bf16)
        for q in range(chunks):
            start = pl.multiple_of(q * chunk_cells + r * REACH, REACH)
            xt[pl.ds(start, REACH), :] = vt[q * REACH : (q + 1) * REACH]
            cent[pl.ds(start, REACH), :] = vc[q * REACH : (q + 1) * REACH]

    repeat(rows, 8, load_row)

    def group_of(slot):
        return [slot in group for group in GROUPS].index(True)

    def moves(k, source, target, count, sender, receiver, toward):
        lines = pl.ds(0, LINES)
        here, there = pl.ds(source, count), pl.ds(target, count)
        return (
            pltpu.make_async_remote_copy(
                src_ref=packets.at[k, here],
                dst_ref=packets.at[k, there],
                send_sem=send_sem.at[k, sender + 1],
                recv_sem=recv_sem.at[k, receiver],
                device_id=device(toward),
                device_id_type=pl.DeviceIdType.MESH,
            ),
            pltpu.make_async_remote_copy(
                src_ref=tails.at[k, here, lines],
                dst_ref=tails.at[k, there, lines],
                send_sem=tail_send_sem.at[k, sender + 1],
                recv_sem=tail_recv_sem.at[k, receiver],
                device_id=device(toward),
                device_id_type=pl.DeviceIdType.MESH,
            ),
        )

    def start(k, slot):
        other = opposite(slot)
        for move in moves(k, 0, BUFFER[other], 1, OFFSETS[slot][0], group_of(other), slot):
            move.start()

    def wait_sent(k, slot):
        count = sum(OFFSETS[other][0] == OFFSETS[slot][0] for other in NEIGHBOURS)
        for move in moves(k, 0, 0, count, OFFSETS[slot][0], 0, EAST):
            move.wait_send()

    def wait_arrived(k, slot):
        group = group_of(slot)
        first = BUFFER[slot]
        for move in moves(k, first, first, len(GROUPS[group]), 0, group, EAST):
            move.wait_recv()

    def unpack(k, slot):
        lanes = slice(slot * slots, (slot + 1) * slots)
        hp = packets[k, BUFFER[slot]]
        hp_all[k, :members, lanes] = hp
        gain_all[k, :members, lanes] = hp
        first_row = lax.broadcasted_iota(jnp.int32, (TAIL, slots), 0) == 0
        shift = jnp.broadcast_to(tails[k, BUFFER[slot], 0:1, :], (TAIL, slots))
        gain_all[k, members : members + TAIL, lanes] = jnp.where(first_row, shift, 0.0).astype(bf16)

    def place(k, slot):
        dy, dx = OFFSETS[slot]
        code = tails[k, BUFFER[slot], 2:3, :].astype(jnp.int32)
        radius = (code & (RADIUS_SPAN - 1)).astype(f32)
        row = (code >> (RADIUS_BITS + COL_BITS)).astype(f32)
        col = ((code >> RADIUS_BITS) & (cols - 1)).astype(f32)
        reach2 = radius * radius
        rate = -2.0 / jnp.maximum(reach2, 1.0)
        return row + float(dy * rows), col + float(dx * cols), reach2, rate, tails[k, BUFFER[slot], 1:2, :]

    def tabulate(k, slot):
        lanes = slice(slot * slots, (slot + 1) * slots)
        row, col, reach2, rate, scale = place(k, slot)
        dx = OFFSETS[slot][1]
        dlat = lax.broadcasted_iota(jnp.int32, (rows, slots), 0).astype(f32) - row
        dlat2 = dlat * dlat
        reach_lat[k, :, lanes] = reach2 - dlat2
        decay_lat[k, :, lanes] = jnp.exp(dlat2 * rate) * scale
        if dx == 0:
            dlon = lax.broadcasted_iota(jnp.int32, (cols, slots), 0).astype(f32) - col
            gap_ref, decay_ref, here = gap_mid, decay_mid, lanes
        else:
            first = 0 if dx < 0 else cols - REACH
            dlon = lax.broadcasted_iota(jnp.int32, (REACH, slots), 0).astype(f32) + float(first) - col
            gap_ref, decay_ref = gap_side, decay_side
            here = slice((slot - 3) * slots, (slot - 2) * slots)
        dlon2 = dlon * dlon
        gap_ref[k, :, here] = dlon2
        decay_ref[k, :, here] = jnp.exp(dlon2 * rate)

    def update(k, q, group, parts, centring):
        cells = pl.ds(pl.multiple_of(q * chunk_cells + group * block, block), block)
        lat_rows = pl.ds(pl.multiple_of(group * GROUP, GROUP), GROUP)
        total = xt[cells, :]
        for first_slot, n_slots, side in parts:
            lanes = slice(first_slot * slots, (first_slot + n_slots) * slots)
            cov = jnp.dot(cent[cells, :], hp_all[k, :, lanes], preferred_element_type=f32)
            if side:
                here = slice((first_slot - 3) * slots, (first_slot - 3 + n_slots) * slots)
                gap, decay = gap_side[k, :, here], decay_side[k, :, here]
            else:
                columns = pl.ds(pl.multiple_of(q * REACH, REACH), REACH)
                gap, decay = gap_mid[k, columns, lanes], decay_mid[k, columns, lanes]
            reach = reach_lat[k, lat_rows, lanes]
            fade = decay_lat[k, lat_rows, lanes]
            pieces = []
            for r in range(GROUP):
                weight = jnp.where(gap <= reach[r : r + 1], decay * fade[r : r + 1], 0.0)
                pieces.append((cov[r * REACH : (r + 1) * REACH] * weight).astype(bf16))
            scaled = jnp.concatenate(pieces, axis=0)
            total += lax.dot_general(
                scaled, gain_all[k, :, lanes], (((1,), (1,)), ((), ())), preferred_element_type=f32
            )
        xt[cells, :] = total
        if centring:
            cent[cells, :] = total.astype(bf16)

    def sweep(k, first_q, n_q, parts, centring=False):
        def step(i):
            q = first_q + i // row_groups
            update(k, q, i % row_groups, parts, centring)

        repeat(n_q * row_groups, min(UNROLL, n_q * row_groups), step)

    def gather(k):
        chosen = order_s[k]

        for s in range(slots):
            hx[pl.ds(s, 1), :] = xt[pl.ds(spot_s[chosen, 0, 0, s], 1), :]

    def aim(k):
        cell = jnp.broadcast_to(cell_ref[order_s[k], 0], (slots, slots))
        at_cell = jnp.transpose(cell.astype(f32)).astype(jnp.int32)
        row_at[...] = (at_cell >> COL_BITS).astype(f32)
        col_at[...] = (at_cell & (cols - 1)).astype(f32)
        hb[...] = hx[...].astype(bf16)
        turned[...] = jnp.transpose(hx[...])

    def look(k, first_slot, n_slots):
        lanes = slice(first_slot * slots, (first_slot + n_slots) * slots)
        cov = jnp.dot(hb[...], hp_all[k, :, lanes], preferred_element_type=f32)
        parts = []
        for i in range(n_slots):
            row, col, reach2, rate, scale = place(k, first_slot + i)
            dlat = row_at[...] - row
            dlon = col_at[...] - col
            gap = dlat * dlat + dlon * dlon
            weight = jnp.where(gap <= reach2, jnp.exp(gap * rate) * scale, 0.0)
            parts.append((cov[:, i * slots : (i + 1) * slots] * weight).astype(bf16))
        scaled = jnp.concatenate(parts, axis=1)
        turned[...] += lax.dot_general(
            gain_all[k, :, lanes], scaled, (((1,), (1,)), ((), ())), preferred_element_type=f32
        )

    def is_live(k):
        return lax.broadcasted_iota(jnp.int32, (1, slots), 1) < count_s[0, 0, order_s[k]]

    def pack(k):
        packets[k, 0] = jnp.where(is_live(k), turned[:members, :], 0.0).astype(bf16)

    def prepare(k):
        chosen = order_s[k]
        prior = turned[...]
        pert = prior[:members]
        mean = prior[members : members + 1]
        var = jnp.sum(pert * pert, axis=0, keepdims=True) * (1.0 / (members - 1))
        error = error_ref[chosen, 0]
        total = var + error
        spread = 1.0 + jnp.sqrt(error / total)
        live = is_live(k)
        scale = jnp.where(live, -1.0 / (((members - 1) * total) * spread), 0.0)
        shift = jnp.where(live, (mean - value_ref[chosen, 0]) * spread, 0.0)
        code = cell_ref[chosen, 0] * RADIUS_SPAN + radius_ref[chosen, 0]
        tails[k, 0, 0:1, :] = shift
        tails[k, 0, 1:2, :] = scale
        tails[k, 0, 2:3, :] = code.astype(f32)

    def send(k):
        for group in SENDS:
            at(group, lambda slot: start(k, slot))

    def receive(k, slots_):
        at([slot for slot in slots_ if OFFSETS[slot][1] <= 0], lambda slot: wait_arrived(k, slot))
        for slot in slots_:
            unpack(k, slot)

    def finish(k):
        at((WEST, NORTH, SOUTH), lambda slot: wait_sent(k, slot))

    def rest(k):
        for slot in NEIGHBOURS:
            tabulate(k, slot)
        sweep(k, 1, chunks - 2, (STACK,), centring=True)
        sweep(k, 0, 1, (STACK, (WEST, 3, True)), centring=True)
        sweep(k, chunks - 1, 1, (STACK, (EAST, 3, True)), centring=True)

    last = batches - 1
    assert batches > 1

    def centre(k):
        unpack(k, 0)
        tabulate(k, 0)
        sweep(k, 0, chunks, ((0, 1, False),))

    def follow(k):
        receive(k, (NORTH, SOUTH, WEST, EAST))
        look(k, 1, 2)
        look(k, WEST, 1)
        look(k, EAST, 1)
        receive(k, CORNERS)
        look(k, WEST + 1, 2)
        look(k, EAST + 1, 2)
        pack(k + 1)
        prepare(k + 1)
        send(k + 1)

    def one_batch(k, carry):
        rest(k - 1)
        gather(k + 1)
        aim(k + 1)
        centre(k)
        look(k, 0, 1)
        finish(k - 1)
        follow(k)
        return carry

    spots.wait()
    gather(0)
    turned[...] = jnp.transpose(hx[...])
    pack(0)
    prepare(0)
    above = (lat + n_lat - 1) // n_lat
    below = (2 * n_lat - 2 - lat) // n_lat
    pl.semaphore_wait(barrier, 2 + 3 * above + 3 * below)
    send(0)
    gather(1)
    aim(1)
    centre(0)
    look(0, 0, 1)
    follow(0)
    lax.fori_loop(1, last, one_batch, 0)

    rest(last - 1)
    centre(last)
    finish(last - 1)
    receive(last, (NORTH,))
    tabulate(last, NORTH)
    sweep(last, 0, chunks, ((NORTH, 1, False),))
    receive(last, (WEST, EAST) + CORNERS[::2])
    for slot in (WEST, EAST) + CORNERS[::2]:
        tabulate(last, slot)
    sweep(last, 0, 1, ((WEST, 1, True), (CORNERS[::2][0], 1, True)))
    sweep(last, chunks - 1, 1, ((EAST, 1, True), (CORNERS[::2][1], 1, True)))
    receive(last, (SOUTH,) + CORNERS[1::2])
    for slot in (SOUTH,) + CORNERS[1::2]:
        tabulate(last, slot)
    sweep(last, 1, chunks - 2, ((SOUTH, 1, False),))
    sweep(last, 0, 1, ((SOUTH, 1, False), (CORNERS[1::2][0], 1, True)))
    sweep(last, chunks - 1, 1, ((SOUTH, 1, False), (CORNERS[1::2][1], 1, True)))

    def store_rows(g):
        lines = []
        for r in range(8):
            pieces = [
                xt[pl.ds(pl.multiple_of(q * chunk_cells + (g * 8 + r) * REACH, REACH), REACH), :]
                for q in range(chunks)
            ]
            v = jnp.transpose(jnp.concatenate(pieces, axis=0))
            lines.append((v[:members] + v[members : members + 1])[None])
        v = jnp.swapaxes(jnp.concatenate(lines, axis=0), 0, 1)
        out_ref[:, pl.ds(pl.multiple_of(g * 8, 8), 8), :] = v

    repeat(rows // 8, 1, store_rows)

    finish(last)


def local(ensemble, obs_value, obs_error, obs_cell, obs_radius, obs_count, batch_order):
    members, levels, rows, cols = ensemble.shape
    batches = obs_cell.shape[0]
    slots = obs_cell.shape[-1]
    assert levels == 1 and cols == LANES and slots == LANES and rows == REACH
    n_lat, n_lon = lax.axis_size("lat"), lax.axis_size("lon")
    padded = -(-members // LANES) * LANES
    cells = rows * cols
    tiles = len(OFFSETS)
    vmem = pl.BlockSpec(memory_space=pltpu.VMEM)
    hbm = pl.BlockSpec(memory_space=pltpu.HBM)
    f32, bf16, i32 = jnp.float32, jnp.bfloat16, jnp.int32
    small = (batches, 1, 1, slots)
    out = pl.pallas_call(
        functools.partial(kernel, (members, rows, cols, slots, batches, n_lat, n_lon)),
        out_shape=pltpu.VMEM((members, rows, cols), f32),
        in_specs=[hbm] * 7,
        out_specs=vmem,
        scratch_shapes=[
            pltpu.VMEM((members * rows, cols), f32),
            pltpu.VMEM(small, f32),
            pltpu.VMEM(small, f32),
            pltpu.VMEM(small, i32),
            pltpu.VMEM(small, i32),
            pltpu.VMEM(small, i32),
            pltpu.SMEM(small, i32),
            pltpu.SMEM((1, 1, batches), i32),
            pltpu.SMEM((batches,), i32),
            pltpu.VMEM((cells, padded), f32),
            pltpu.VMEM((cells, padded), bf16),
            pltpu.VMEM((slots, padded), f32),
            pltpu.VMEM((slots, padded), bf16),
            pltpu.VMEM((slots, slots), f32),
            pltpu.VMEM((slots, slots), f32),
            pltpu.VMEM((padded, slots), f32),
            pltpu.VMEM((batches, tiles, members, slots), bf16),
            pltpu.VMEM((batches, tiles, 8, slots), f32),
            pltpu.VMEM((batches, padded, tiles * slots), bf16),
            pltpu.VMEM((batches, padded, tiles * slots), bf16),
            pltpu.VMEM((batches, rows, tiles * slots), f32),
            pltpu.VMEM((batches, rows, tiles * slots), f32),
            pltpu.VMEM((batches, cols, 3 * slots), f32),
            pltpu.VMEM((batches, cols, 3 * slots), f32),
            pltpu.VMEM((batches, REACH, 6 * slots), f32),
            pltpu.VMEM((batches, REACH, 6 * slots), f32),
            pltpu.SemaphoreType.DMA((8,)),
            pltpu.SemaphoreType.DMA((batches, 3)),
            pltpu.SemaphoreType.DMA((batches, len(GROUPS))),
            pltpu.SemaphoreType.DMA((batches, 3)),
            pltpu.SemaphoreType.DMA((batches, len(GROUPS))),
        ],
        compiler_params=pltpu.CompilerParams(
            collective_id=0, has_side_effects=True, vmem_limit_bytes=58 * 1024 * 1024
        ),
    )(
        ensemble.reshape(members * rows, cols),
        obs_value,
        obs_error,
        obs_cell,
        obs_radius,
        jnp.transpose(obs_count, (1, 2, 0)),
        batch_order,
    )
    return out.reshape(ensemble.shape)


def solution(mesh):
    return jax.shard_map(
        local,
        mesh=mesh,
        in_specs=(
            P(None, None, "lat", "lon"),
            P(None, "lat", "lon", None),
            P(None, "lat", "lon", None),
            P(None, "lat", "lon", None),
            P(None, "lat", "lon", None),
            P(None, "lat", "lon"),
            P(),
        ),
        out_specs=P(None, None, "lat", "lon"),
        check_vma=False,
    )
```
